32 devices in a mesh: gx: 8 (over z, x), gy: 4 (over y, core).
Axes of the slice: x: 2, y: 2, z: 4, core: 2. Of those that a mesh axis runs over, the one named last changes fastest.
Arguments:
- impedance: bfloat16 [8, 4, 1024, 1024], P('gx', 'gy'), may hold values from -0.1875 to 0.1875
- rebuild_map: bfloat16 [8, 4, 256, 1024], P('gx', 'gy'), may hold values from -0.1875 to 0.1875
- left_trace: bfloat16 [8, 4, 512, 512], P('gx', 'gy'), may hold values from -6 to 6
- lower_trace: bfloat16 [8, 4, 512, 512], P('gx', 'gy'), may hold values from -6 to 6
- cell_kind: int32 [128, 64], P('gx', 'gy'), may hold values from 0 to 15
- kind_wavenum: float32 [16], replicated, may hold values from 0.5 to 3
Outputs:
- right_trace: bfloat16 [8, 4, 512, 512], P('gx', 'gy')
- upper_trace: bfloat16 [8, 4, 512, 512], P('gx', 'gy')
- residual: float32 [128, 64, 512], P('gx', 'gy')
The draws below stay inside these ranges and needn't reach their ends.
All inputs are finite; a program needn't handle non-finite values.
Results may differ from the reference program's by a relative error of at most 0.0064.
Values may be sent and summed in bfloat16 or wider, within the bound.
No kernel may reach another device: no remote copies, remote signals or barrier semaphores. Data moves between devices by JAX's collectives and lax.ppermute only.
A program may use at most 64 MiB of HBM per device.

```python
import math
import jax
import jax.numpy as jnp
from jax import lax

TRACE = 512
SRC = 512
CX = 16
CY = 16
STEPS = 4
KINDS = 16
NX = 128
NY = 64
N_GX = 8
N_GY = 4


def with_ends(array, own_key, low, top_value):
    longest = array.shape.index(max(array.shape))
    spots = []
    for shift in (0, 1):
        where = [jax.random.randint(jax.random.fold_in(own_key, axis), (), 0, length) for axis, length in enumerate(array.shape)]
        where[longest] = (where[longest] + shift) % array.shape[longest]
        spots.append(tuple(where))
    return array.at[spots[0]].set(low).at[spots[1]].set(top_value)


def block_scale(rng, dims, shards, smallest, largest):
    gain = 1.0
    for axis_at, blocks in shards:
        draws = jax.random.uniform(jax.random.fold_in(jax.random.fold_in(rng, 6), axis_at), (blocks,), jnp.float32, smallest / len(shards), largest / len(shards))
        gain = gain * jnp.repeat(jnp.exp(draws), dims[axis_at] // blocks).reshape((-1,) + (1,) * (len(dims) - 1 - axis_at))
    return gain


def noise(key, shape, deviation, bound, pieces=(), dtype=jnp.bfloat16):
    result = deviation * jax.random.normal(key, shape, jnp.float32)
    if pieces:
        result = result * block_scale(key, shape, pieces, -0.22, 0.18)
    return jnp.clip(result, -bound, bound).astype(dtype)


def setup_inputs(seed: int = 0) -> dict:
    streams_of = jax.random.split(jax.random.key(seed), 7)
    return {
        "impedance": noise(streams_of[0], (N_GX, N_GY, 2 * TRACE, 2 * TRACE), (2 * TRACE) ** -0.5, 0.1875, ((0, 8), (1, 4))),
        "rebuild_map": noise(streams_of[1], (N_GX, N_GY, CX * CY, 2 * TRACE), (2 * TRACE) ** -0.5, 0.1875, ((0, 8), (1, 4))),
        "left_trace": noise(streams_of[2], (N_GX, N_GY, TRACE, SRC), 1.0, 6.0, ((0, 8), (1, 4))),
        "lower_trace": noise(streams_of[3], (N_GX, N_GY, TRACE, SRC), 1.0, 6.0, ((0, 8), (1, 4))),
        "cell_kind": with_ends(jax.random.randint(streams_of[4], (NX, NY), 0, KINDS), jax.random.fold_in(streams_of[4], 1), 0, KINDS - 1).astype(jnp.int32),
        "kind_wavenum": jnp.clip(jnp.exp(jax.random.uniform(streams_of[5], (KINDS,), jnp.float32, math.log(0.5), math.log(3.0))), 0.5, 3.0),
    }


def advance_all(impedance, left_in, lower_in):
    def per_row(items):
        mapping, left_row, lower_row = items
        stacked = jnp.concatenate([left_row, lower_row], axis=1).astype(jnp.float32)
        outgoing = jnp.einsum("gij,gjs->gis", mapping.astype(jnp.float32), stacked, precision=lax.Precision.HIGHEST)
        return outgoing.astype(jnp.bfloat16)

    outgoing = lax.map(per_row, (impedance, left_in, lower_in))
    return outgoing[:, :, :TRACE], outgoing[:, :, TRACE:]


def rebuild_all(rebuild_map, left_in, lower_in):
    def per_row(items):
        mapping, left_row, lower_row = items
        stacked = jnp.concatenate([left_row, lower_row], axis=1).astype(jnp.float32)
        return jnp.einsum("gcj,gjs->gcs", mapping.astype(jnp.float32), stacked, precision=lax.Precision.HIGHEST)

    return lax.map(per_row, (rebuild_map, left_in, lower_in))


def reference(impedance, rebuild_map, left_trace, lower_trace, cell_kind, kind_wavenum):
    left_in, lower_in = left_trace, lower_trace
    right_out, upper_out = left_in, lower_in
    for sweep_step in range(STEPS):
        right_out, upper_out = advance_all(impedance, left_in, lower_in)
        if sweep_step + 1 < STEPS:
            left_in = jnp.concatenate([jnp.zeros_like(right_out[:1]), right_out[:-1]], axis=0)
            lower_in = jnp.concatenate([jnp.zeros_like(upper_out[:, :1]), upper_out[:, :-1]], axis=1)
    tiles = rebuild_all(rebuild_map, left_in, lower_in)
    volume = tiles.reshape(N_GX, N_GY, CX, CY, SRC).transpose(0, 2, 1, 3, 4).reshape(NX, NY, SRC)
    padded = jnp.pad(volume, ((1, 1), (1, 1), (0, 0)))
    beside = padded[2:, 1:-1] + padded[:-2, 1:-1] + padded[1:-1, 2:] + padded[1:-1, :-2]
    wavenum = kind_wavenum[cell_kind]
    residual = beside - 4.0 * volume + wavenum[:, :, None] * volume
    return right_out, upper_out, residual
```

```python
import jax
import jax.numpy as jnp
from jax import lax
from jax.sharding import PartitionSpec as P

STEPS = 4
CHUNKS = 2


def shifted(block, axis, step):
    count = lax.axis_size(axis)
    end = count - 1 if step > 0 else 0
    block = jnp.where(lax.axis_index(axis) == end, jnp.zeros_like(block), block)
    return lax.ppermute(block, axis, [(i, (i + step) % count) for i in range(count)])


def advance(mapping, left_in, lower_in):
    stacked = jnp.concatenate([left_in, lower_in], axis=0)
    outgoing = jnp.dot(mapping, stacked, preferred_element_type=jnp.float32).astype(jnp.bfloat16)
    rows = left_in.shape[0]
    return (outgoing[:rows], outgoing[rows:])


def per_device(impedance, rebuild_map, left_trace, lower_trace, cell_kind, kind_wavenum):
    mapping = impedance[0, 0]
    sources = left_trace.shape[3]
    width = sources // CHUNKS
    left_in = [left_trace[0, 0, :, c * width : (c + 1) * width] for c in range(CHUNKS)]
    lower_in = [lower_trace[0, 0, :, c * width : (c + 1) * width] for c in range(CHUNKS)]
    for _ in range(STEPS - 1):
        for c in range(CHUNKS):
            right, upper = advance(mapping, left_in[c], lower_in[c])
            left_in[c] = shifted(right, "gx", 1)
            lower_in[c] = shifted(upper, "gy", 1)
    left_in = jnp.concatenate(left_in, axis=1)
    lower_in = jnp.concatenate(lower_in, axis=1)
    cells_x, cells_y = cell_kind.shape
    stacked = jnp.concatenate([left_in, lower_in], axis=0)
    volume = jnp.dot(rebuild_map[0, 0], stacked, preferred_element_type=jnp.float32).reshape(
        cells_x, cells_y, sources
    )
    low = volume.astype(jnp.bfloat16)
    from_left = shifted(low[-1], "gx", 1)
    from_right = shifted(low[0], "gx", -1)
    from_below = shifted(low[:, -1], "gy", 1)
    from_above = shifted(low[:, 0], "gy", -1)
    right_out, upper_out = advance(mapping, left_in, lower_in)
    f32 = jnp.float32
    along_x = jnp.concatenate([from_left[None].astype(f32), volume, from_right[None].astype(f32)], axis=0)
    along_y = jnp.concatenate([from_below[:, None].astype(f32), volume, from_above[:, None].astype(f32)], axis=1)
    beside = along_x[2:] + along_x[:-2] + along_y[:, 2:] + along_y[:, :-2]
    kind_ids = jnp.arange(kind_wavenum.shape[0], dtype=jnp.int32)
    wavenum = jnp.sum(
        jnp.where(
            cell_kind[:, :, None] == kind_ids[None, None, :],
            kind_wavenum[None, None, :],
            jnp.float32(0.0),
        ),
        axis=-1,
    )
    residual = beside - 4.0 * volume + wavenum[:, :, None] * volume
    return (right_out[None, None], upper_out[None, None], residual)


def solution(mesh):
    return jax.shard_map(
        per_device,
        mesh=mesh,
        in_specs=(
            P("gx", "gy", None, None),
            P("gx", "gy", None, None),
            P("gx", "gy", None, None),
            P("gx", "gy", None, None),
            P("gx", "gy"),
            P(),
        ),
        out_specs=(P("gx", "gy", None, None), P("gx", "gy", None, None), P("gx", "gy", None)),
        check_vma=False,
    )
```

```python
import functools

import jax
import jax.numpy as jnp
from jax import lax
from jax.experimental import pallas as pl
from jax.experimental.pallas import tpu as pltpu
from jax.sharding import PartitionSpec as P

STEPS = 4
CHUNKS = 2
F32 = jnp.float32
BF16 = jnp.bfloat16
VMEM = pl.BlockSpec(memory_space=pltpu.VMEM)
HBM = pl.BlockSpec(memory_space=pltpu.HBM)


def around(block, axis):
    count = lax.axis_size(axis)
    return lax.ppermute(block, axis, [(i, (i + 1) % count) for i in range(count)])


def swapped(block, axis, first):
    count = lax.axis_size(axis)
    pairs = [((first + i) % count, (first + (i ^ 1)) % count) for i in range(count)]
    return lax.ppermute(block, axis, sorted(pairs))


def is_last(axis):
    return lax.axis_index(axis) == lax.axis_size(axis) - 1


PARAMS = pltpu.CompilerParams(vmem_limit_bytes=6 * 2**20)


def cost(flops, moved):
    return pl.CostEstimate(flops=flops, bytes_accessed=moved, transcendentals=0)


def product(weights, left, lower):
    half = left.shape[0]
    return jnp.dot(weights[:, :half], left[...], preferred_element_type=F32) + jnp.dot(
        weights[:, half:], lower[...], preferred_element_type=F32
    )


def first_right_kernel(base, width, z_hbm, left_hbm, lower_hbm, out, z_top, left, lower, sem):
    rows = z_top.shape[0]
    block = rows // 2
    loads = [
        pltpu.make_async_copy(left_hbm.at[:, pl.ds(base, width)], left, sem.at[0]),
        pltpu.make_async_copy(lower_hbm.at[:, pl.ds(base, width)], lower, sem.at[1]),
    ]
    parts = [
        pltpu.make_async_copy(z_hbm.at[pl.ds(r * block, block)], z_top.at[pl.ds(r * block, block)], sem.at[2 + r])
        for r in range(2)
    ]
    for copy in loads + parts:
        copy.start()
    for copy in loads:
        copy.wait()
    at_end = is_last("gx")
    for r in range(2):
        parts[r].wait()
        here = pl.ds(r * block, block)
        out[here] = jnp.where(at_end, 0.0, product(z_top.at[here], left, lower)).astype(BF16)


def first_right(z, left, lower, base, width):
    trace = left.shape[0]
    vmem = lambda *shape: jax.ShapeDtypeStruct(shape, BF16)
    return pl.pallas_call(
        functools.partial(first_right_kernel, base, width),
        out_shape=(vmem(trace, width), vmem(trace, 2 * trace), vmem(trace, width), vmem(trace, width)),
        in_specs=[HBM, HBM, HBM],
        out_specs=(VMEM,) * 4,
        scratch_shapes=[pltpu.SemaphoreType.DMA((4,))],
        cost_estimate=cost(4 * trace * trace * width, 3 * trace * trace),
        compiler_params=PARAMS,
        name="first_right",
    )(z, left, lower)


def first_upper_kernel(z_hbm, left, lower, out, z_low, sem):
    rows = z_low.shape[0]
    block = rows // 2
    parts = [
        pltpu.make_async_copy(z_hbm.at[pl.ds(rows + r * block, block)], z_low.at[pl.ds(r * block, block)], sem.at[r])
        for r in range(2)
    ]
    for copy in parts:
        copy.start()
    at_end = is_last("gy")
    for r in range(2):
        parts[r].wait()
        here = pl.ds(r * block, block)
        out[here] = jnp.where(at_end, 0.0, product(z_low.at[here], left, lower)).astype(BF16)


def first_upper(z, left, lower):
    trace, width = left.shape
    vmem = lambda *shape: jax.ShapeDtypeStruct(shape, BF16)
    return pl.pallas_call(
        first_upper_kernel,
        out_shape=(vmem(trace, width), vmem(trace, 2 * trace)),
        in_specs=[HBM, VMEM, VMEM],
        out_specs=(VMEM,) * 2,
        scratch_shapes=[pltpu.SemaphoreType.DMA((2,))],
        cost_estimate=cost(4 * trace * trace * width, 3 * trace * trace),
        compiler_params=PARAMS,
        name="first_upper",
    )(z, left, lower)


def write_both(z_top, z_low, left, lower, right, upper):
    half = left.shape[0] // 2
    for axis, z, out in (("gx", z_top, right), ("gy", z_low, upper)):
        at_end = is_last(axis)
        for r in range(2):
            here = pl.ds(r * half, half)
            out[here] = jnp.where(at_end, 0.0, product(z.at[here], left, lower)).astype(BF16)


def both_loading_kernel(base, z_top, z_low, left_hbm, lower_hbm, right, upper, left, lower, sem):
    width = left.shape[1]
    loads = [
        pltpu.make_async_copy(left_hbm.at[:, pl.ds(base, width)], left, sem.at[0]),
        pltpu.make_async_copy(lower_hbm.at[:, pl.ds(base, width)], lower, sem.at[1]),
    ]
    for copy in loads:
        copy.start()
    for copy in loads:
        copy.wait()
    write_both(z_top, z_low, left, lower, right, upper)


def both_loading(z_top, z_low, left, lower, base, width):
    trace = left.shape[0]
    out = jax.ShapeDtypeStruct((trace, width), BF16)
    return pl.pallas_call(
        functools.partial(both_loading_kernel, base),
        out_shape=(out, out),
        in_specs=[VMEM, VMEM, HBM, HBM],
        out_specs=(VMEM, VMEM),
        scratch_shapes=[
            pltpu.VMEM((trace, width), BF16),
            pltpu.VMEM((trace, width), BF16),
            pltpu.SemaphoreType.DMA((2,)),
        ],
        cost_estimate=cost(8 * trace * trace * width, 4 * trace * trace),
        compiler_params=PARAMS,
        name="both_loading",
    )(z_top, z_low, left, lower)


def both(z_top, z_low, left, lower):
    trace, width = left.shape
    out = jax.ShapeDtypeStruct((trace, width), BF16)
    return pl.pallas_call(
        write_both,
        out_shape=(out, out),
        in_specs=[VMEM] * 4,
        out_specs=(VMEM, VMEM),
        cost_estimate=cost(8 * trace * trace * width, 4 * trace * trace),
        compiler_params=PARAMS,
        name="both",
    )(z_top, z_low, left, lower)


def volume_kernel(weights, left, lower, volume):
    volume[...] = product(weights, left, lower)


def volume_of(weights, left, lower):
    width = left.shape[1]
    return pl.pallas_call(
        volume_kernel,
        out_shape=jax.ShapeDtypeStruct((weights.shape[0], width), F32),
        in_specs=[VMEM] * 3,
        out_specs=VMEM,
        cost_estimate=cost(2 * weights.size * width, weights.size),
        compiler_params=PARAMS,
        name="volume",
    )(weights, left, lower)


def edges_kernel(cells_y, weights, left, lower, done, volume, x_pair, x_cross, y_pair, y_cross):
    cells = weights.shape[0]
    old = done.shape[1]
    volume[...] = product(weights, left, lower)
    even_x = lax.rem(lax.axis_index("gx"), 2) == 0
    even_y = lax.rem(lax.axis_index("gy"), 2) == 0
    for where, block in ((pl.ds(0, old), done), (pl.ds(old, volume.shape[1]), volume)):
        first = block[pl.ds(0, cells_y)]
        last = block[pl.ds(cells - cells_y, cells_y)]
        x_pair[:, where] = jnp.where(even_x, last, first).astype(BF16)
        x_cross[:, where] = jnp.where(even_x, first, last).astype(BF16)
        first = jnp.concatenate([block[pl.ds(x, 1)] for x in range(0, cells, cells_y)], axis=0)
        last = jnp.concatenate([block[pl.ds(x + cells_y - 1, 1)] for x in range(0, cells, cells_y)], axis=0)
        y_pair[:, where] = jnp.where(even_y, last, first).astype(BF16)
        y_cross[:, where] = jnp.where(even_y, first, last).astype(BF16)


def edges_of(weights, left, lower, done, cells_y):
    cells = weights.shape[0]
    width = left.shape[1]
    total = width + done.shape[1]
    line = lambda n: jax.ShapeDtypeStruct((n, total), BF16)
    return pl.pallas_call(
        functools.partial(edges_kernel, cells_y),
        out_shape=(
            jax.ShapeDtypeStruct((cells, width), F32),
            line(cells_y),
            line(cells_y),
            line(cells // cells_y),
            line(cells // cells_y),
        ),
        in_specs=[VMEM] * 4,
        out_specs=(VMEM,) * 5,
        cost_estimate=cost(2 * weights.size * width, weights.size),
        compiler_params=PARAMS,
        name="edges",
    )(weights, left, lower, done)


def last_kernel(base, z_top, z_low, left, lower, *refs):
    right_hbm, upper_hbm, right, upper, sem = refs[-5:]
    width = left.shape[1]
    half = left.shape[0] // 2
    copies = []
    for z, out, out_hbm in ((z_top, right, right_hbm), (z_low, upper, upper_hbm)):
        for r in range(2):
            here = pl.ds(r * half, half)
            out[here] = product(z.at[here], left, lower).astype(BF16)
            copies.append(
                pltpu.make_async_copy(out.at[here], out_hbm.at[here, pl.ds(base, width)], sem.at[len(copies)])
            )
            copies[-1].start()
    for copy in copies:
        copy.wait()


def last(z_top, z_low, left, lower, before, base, total):
    trace, width = left.shape
    out = jax.ShapeDtypeStruct((trace, total), BF16)
    return pl.pallas_call(
        functools.partial(last_kernel, base),
        out_shape=(out, out),
        in_specs=[VMEM] * 4 + [HBM] * len(before),
        out_specs=(HBM, HBM),
        scratch_shapes=[
            pltpu.VMEM((trace, width), BF16),
            pltpu.VMEM((trace, width), BF16),
            pltpu.SemaphoreType.DMA((4,)),
        ],
        input_output_aliases={4 + k: k for k in range(len(before))},
        cost_estimate=cost(8 * trace * trace * width, 4 * trace * trace),
        compiler_params=PARAMS,
        name="last",
    )(z_top, z_low, left, lower, *before)


def beside(axis, pair, cross):
    place = lax.axis_index(axis)
    even = lax.rem(place, 2) == 0
    pair, cross = pair[...].astype(F32), cross[...].astype(F32)
    before = jnp.where(place == 0, 0.0, jnp.where(even, cross, pair))
    after = jnp.where(is_last(axis), 0.0, jnp.where(even, pair, cross))
    return before, after


def residual_kernel(cells_y, wavenum, *refs):
    volumes = refs[:-5]
    x_pair, x_cross, y_pair, y_cross, out = refs[-5:]
    cells = volumes[0].shape[0]
    start = 0
    for volume in volumes:
        width = volume.shape[1]
        where = pl.ds(start, width)
        start += width
        before_x, after_x = beside("gx", x_pair.at[:, where], x_cross.at[:, where])
        before_y, after_y = beside("gy", y_pair.at[:, where], y_cross.at[:, where])
        place = lax.broadcasted_iota(jnp.int32, (cells_y, width), 0)
        for x in range(cells // cells_y):
            here = volume[pl.ds(x * cells_y, cells_y)]
            left = volume[pl.ds((x - 1) * cells_y, cells_y)] if x else before_x
            right = volume[pl.ds((x + 1) * cells_y, cells_y)] if (x + 1) * cells_y < cells else after_x
            below = jnp.where(place == 0, before_y[x : x + 1], pltpu.roll(here, 1, 0))
            above = jnp.where(place == cells_y - 1, after_y[x : x + 1], pltpu.roll(here, cells_y - 1, 0))
            scale = wavenum[pl.ds(x * cells_y, cells_y)][:, :1]
            out[x, :, where] = (right + left + above + below - 4.0 * here) + scale * here


def residual_of(wavenum, volumes, halos, cells_y):
    cells = volumes[0].shape[0]
    total = halos[0].shape[1]
    return pl.pallas_call(
        functools.partial(residual_kernel, cells_y),
        out_shape=jax.ShapeDtypeStruct((cells // cells_y, cells_y, total), F32),
        in_specs=[VMEM] * (5 + len(volumes)),
        out_specs=VMEM,
        cost_estimate=cost(10 * cells * total, 8 * cells * total),
        compiler_params=PARAMS,
        name="residual",
    )(wavenum, *volumes, *halos)


def per_device(impedance, rebuild_map, left_trace, lower_trace, cell_kind, kind_wavenum):
    z = pltpu.with_memory_space_constraint(impedance[0, 0], pltpu.HBM)
    weights = rebuild_map[0, 0]
    left_all = pltpu.with_memory_space_constraint(left_trace[0, 0], pltpu.HBM)
    lower_all = pltpu.with_memory_space_constraint(lower_trace[0, 0], pltpu.HBM)
    sources = left_all.shape[1]
    width = sources // CHUNKS
    cells_x, cells_y = cell_kind.shape
    left_in, lower_in = [None] * CHUNKS, [None] * CHUNKS
    for step in range(STEPS - 1):
        for c in range(CHUNKS):
            if step == 0 and c == 0:
                right, z_top, left_first, lower_first = first_right(z, left_all, lower_all, 0, width)
                left_in[c] = around(right, "gx")
                upper, z_low = first_upper(z, left_first, lower_first)
            else:
                if step == 0:
                    right, upper = both_loading(z_top, z_low, left_all, lower_all, c * width, width)
                else:
                    right, upper = both(z_top, z_low, left_in[c], lower_in[c])
                left_in[c] = around(right, "gx")
            lower_in[c] = around(upper, "gy")

    kind_ids = jnp.arange(kind_wavenum.shape[0], dtype=jnp.int32)
    wavenum = jnp.sum(
        jnp.where(cell_kind[:, :, None] == kind_ids[None, None, :], kind_wavenum[None, None, :], F32(0.0)),
        axis=-1,
    )
    wavenum = jnp.broadcast_to(wavenum.reshape(cells_x * cells_y, 1), (cells_x * cells_y, 128))

    volume_a = volume_of(weights, left_in[0], lower_in[0])
    outs = last(z_top, z_low, left_in[0], lower_in[0], (), 0, sources)
    volume_a, left_in[1], lower_in[1], *outs = lax.optimization_barrier((volume_a, left_in[1], lower_in[1], *outs))
    volume_b, x_pair, x_cross, y_pair, y_cross = edges_of(weights, left_in[1], lower_in[1], volume_a, cells_y)
    halos = (
        swapped(x_pair, "gx", 0),
        swapped(x_cross, "gx", 1),
        swapped(y_pair, "gy", 0),
        swapped(y_cross, "gy", 1),
    )
    right_out, upper_out = last(z_top, z_low, left_in[1], lower_in[1], outs, width, sources)
    residual = residual_of(wavenum, (volume_a, volume_b), halos, cells_y)
    return (right_out[None, None], upper_out[None, None], residual)


def solution(mesh):
    return jax.shard_map(
        per_device,
        mesh=mesh,
        in_specs=(
            P("gx", "gy", None, None),
            P("gx", "gy", None, None),
            P("gx", "gy", None, None),
            P("gx", "gy", None, None),
            P("gx", "gy"),
            P(),
        ),
        out_specs=(P("gx", "gy", None, None), P("gx", "gy", None, None), P("gx", "gy", None)),
        check_vma=False,
    )
```

```python
import functools

import jax
import jax.numpy as jnp
from jax import lax
from jax.experimental import pallas as pl
from jax.experimental.pallas import tpu as pltpu
from jax.sharding import PartitionSpec as P

STEPS = 4
CHUNKS = 2
F32 = jnp.float32
BF16 = jnp.bfloat16
VMEM = pl.BlockSpec(memory_space=pltpu.VMEM)
HBM = pl.BlockSpec(memory_space=pltpu.HBM)


def around(block, axis):
    count = lax.axis_size(axis)
    return lax.ppermute(block, axis, [(i, (i + 1) % count) for i in range(count)])


def swapped(block, axis, first):
    names = ("gx", "gy")
    along = names.index(axis)
    sizes = tuple(lax.axis_size(name) for name in names)
    pairs = []
    for place in range(sizes[0] * sizes[1]):
        where = [place // sizes[1], place % sizes[1]]
        mate = first + ((where[along] - first) ^ 1)
        if 0 <= mate < sizes[along]:
            where[along] = mate
        else:
            where[1 - along] ^= 1
        pairs.append((place, where[0] * sizes[1] + where[1]))
    return lax.ppermute(block, names, pairs)


def is_last(axis):
    return lax.axis_index(axis) == lax.axis_size(axis) - 1


PARAMS = pltpu.CompilerParams(vmem_limit_bytes=6 * 2**20)


def cost(flops, moved):
    return pl.CostEstimate(flops=int(flops), bytes_accessed=int(moved), transcendentals=0)


def product(weights, left, lower):
    half = left.shape[0]
    return jnp.dot(weights[:, :half], left[...], preferred_element_type=F32) + jnp.dot(
        weights[:, half:], lower[...], preferred_element_type=F32
    )


def first_right_kernel(base, width, z_hbm, left_hbm, lower_hbm, out, z_top, left, lower, sem):
    rows = z_top.shape[0]
    block = rows // 2
    loads = [
        pltpu.make_async_copy(left_hbm.at[:, pl.ds(base, width)], left, sem.at[0]),
        pltpu.make_async_copy(lower_hbm.at[:, pl.ds(base, width)], lower, sem.at[1]),
    ]
    parts = [
        pltpu.make_async_copy(z_hbm.at[pl.ds(r * block, block)], z_top.at[pl.ds(r * block, block)], sem.at[2 + r])
        for r in range(2)
    ]
    for copy in loads + parts:
        copy.start()
    for copy in loads:
        copy.wait()
    at_end = is_last("gx")
    for r in range(2):
        parts[r].wait()
        here = pl.ds(r * block, block)
        out[here] = jnp.where(at_end, 0.0, product(z_top.at[here], left, lower)).astype(BF16)


def first_right(z, left, lower, base, width):
    trace = left.shape[0]
    vmem = lambda *shape: jax.ShapeDtypeStruct(shape, BF16)
    return pl.pallas_call(
        functools.partial(first_right_kernel, base, width),
        out_shape=(vmem(trace, width), vmem(trace, 2 * trace), vmem(trace, width), vmem(trace, width)),
        in_specs=[HBM, HBM, HBM],
        out_specs=(VMEM,) * 4,
        scratch_shapes=[pltpu.SemaphoreType.DMA((4,))],
        cost_estimate=cost(4 * trace * trace * width, 4 * trace * trace + 6 * trace * width),
        compiler_params=PARAMS,
        name="first_right",
    )(z, left, lower)


def first_upper_kernel(z_hbm, left, lower, out, z_low, sem):
    rows = z_low.shape[0]
    block = rows // 2
    parts = [
        pltpu.make_async_copy(z_hbm.at[pl.ds(rows + r * block, block)], z_low.at[pl.ds(r * block, block)], sem.at[r])
        for r in range(2)
    ]
    for copy in parts:
        copy.start()
    at_end = is_last("gy")
    for r in range(2):
        parts[r].wait()
        here = pl.ds(r * block, block)
        out[here] = jnp.where(at_end, 0.0, product(z_low.at[here], left, lower)).astype(BF16)


def first_upper(z, left, lower):
    trace, width = left.shape
    vmem = lambda *shape: jax.ShapeDtypeStruct(shape, BF16)
    return pl.pallas_call(
        first_upper_kernel,
        out_shape=(vmem(trace, width), vmem(trace, 2 * trace)),
        in_specs=[HBM, VMEM, VMEM],
        out_specs=(VMEM,) * 2,
        scratch_shapes=[pltpu.SemaphoreType.DMA((2,))],
        cost_estimate=cost(4 * trace * trace * width, 4 * trace * trace + 6 * trace * width),
        compiler_params=PARAMS,
        name="first_upper",
    )(z, left, lower)


def part_kernel(axis, z, left, lower, out):
    half = left.shape[0] // 2
    at_end = is_last(axis)
    for r in range(2):
        here = pl.ds(r * half, half)
        out[here] = jnp.where(at_end, 0.0, product(z.at[here], left, lower)).astype(BF16)


def part(axis, z, left, lower):
    trace, width = left.shape
    return pl.pallas_call(
        functools.partial(part_kernel, axis),
        out_shape=jax.ShapeDtypeStruct((trace, width), BF16),
        in_specs=[VMEM] * 3,
        out_specs=VMEM,
        cost_estimate=cost(4 * trace * trace * width, 4 * trace * trace + 6 * trace * width),
        compiler_params=PARAMS,
        name="part",
    )(z, left, lower)


def part_loading_kernel(axis, base, z, left_hbm, lower_hbm, out, left, lower, sem):
    width = left.shape[1]
    loads = [
        pltpu.make_async_copy(left_hbm.at[:, pl.ds(base, width)], left, sem.at[0]),
        pltpu.make_async_copy(lower_hbm.at[:, pl.ds(base, width)], lower, sem.at[1]),
    ]
    for copy in loads:
        copy.start()
    for copy in loads:
        copy.wait()
    part_kernel(axis, z, left, lower, out)


def part_loading(axis, z, left, lower, base, width):
    trace = left.shape[0]
    block = jax.ShapeDtypeStruct((trace, width), BF16)
    return pl.pallas_call(
        functools.partial(part_loading_kernel, axis, base),
        out_shape=(block,) * 3,
        in_specs=[VMEM, HBM, HBM],
        out_specs=(VMEM,) * 3,
        scratch_shapes=[pltpu.SemaphoreType.DMA((2,))],
        cost_estimate=cost(4 * trace * trace * width, 4 * trace * trace + 6 * trace * width),
        compiler_params=PARAMS,
        name="part_loading",
    )(z, left, lower)


def wavenum_kernel(table, kinds, out):
    cells_x, cells_y = kinds.shape
    kind = kinds[...]
    value = jnp.zeros(kind.shape, F32)
    for k in range(table.shape[0]):
        value = jnp.where(kind == k, table[k], value)
    shape = (cells_y, cells_y)
    diagonal = lax.broadcasted_iota(jnp.int32, shape, 0) == lax.broadcasted_iota(jnp.int32, shape, 1)
    for x in range(cells_x):
        column = jnp.sum(jnp.where(diagonal, value[x : x + 1], 0.0), axis=1, keepdims=True)
        out[pl.ds(x * cells_y, cells_y)] = jnp.broadcast_to(column, (cells_y, out.shape[1]))


def wavenum_of(table, kinds):
    return pl.pallas_call(
        wavenum_kernel,
        out_shape=jax.ShapeDtypeStruct((kinds.size, 128), F32),
        in_specs=[pl.BlockSpec(memory_space=pltpu.SMEM), VMEM],
        out_specs=VMEM,
        compiler_params=PARAMS,
        name="wavenum",
    )(table, kinds)


def volume_kernel(weights, left, lower, volume):
    volume[...] = product(weights, left, lower)


def volume_of(weights, left, lower):
    width = left.shape[1]
    return pl.pallas_call(
        volume_kernel,
        out_shape=jax.ShapeDtypeStruct((weights.shape[0], width), F32),
        in_specs=[VMEM] * 3,
        out_specs=VMEM,
        cost_estimate=cost(2 * weights.size * width, 2 * weights.size + 4 * weights.shape[1] * width),
        compiler_params=PARAMS,
        name="volume",
    )(weights, left, lower)


def edges_kernel(cells_y, weights, left, lower, done, volume, x_pair, x_cross, y_pair, y_cross):
    cells = weights.shape[0]
    old = done.shape[1]
    volume[...] = product(weights, left, lower)
    even_x = lax.rem(lax.axis_index("gx"), 2) == 0
    even_y = lax.rem(lax.axis_index("gy"), 2) == 0
    for where, block in ((pl.ds(0, old), done), (pl.ds(old, volume.shape[1]), volume)):
        first = block[pl.ds(0, cells_y)]
        last = block[pl.ds(cells - cells_y, cells_y)]
        x_pair[:, where] = jnp.where(even_x, last, first).astype(BF16)
        x_cross[:, where] = jnp.where(even_x, first, last).astype(BF16)
        first = jnp.concatenate([block[pl.ds(x, 1)] for x in range(0, cells, cells_y)], axis=0)
        last = jnp.concatenate([block[pl.ds(x + cells_y - 1, 1)] for x in range(0, cells, cells_y)], axis=0)
        y_pair[:, where] = jnp.where(even_y, last, first).astype(BF16)
        y_cross[:, where] = jnp.where(even_y, first, last).astype(BF16)


def edges_of(weights, left, lower, done, cells_y):
    cells = weights.shape[0]
    width = left.shape[1]
    total = width + done.shape[1]
    line = lambda n: jax.ShapeDtypeStruct((n, total), BF16)
    return pl.pallas_call(
        functools.partial(edges_kernel, cells_y),
        out_shape=(
            jax.ShapeDtypeStruct((cells, width), F32),
            line(cells_y),
            line(cells_y),
            line(cells // cells_y),
            line(cells // cells_y),
        ),
        in_specs=[VMEM] * 4,
        out_specs=(VMEM,) * 5,
        cost_estimate=cost(2 * weights.size * width, 2 * weights.size + 4 * weights.shape[1] * width),
        compiler_params=PARAMS,
        name="edges",
    )(weights, left, lower, done)


def last_kernel(z_top, z_low, left, lower, right_hbm, upper_hbm, right, upper, sem):
    width = left.shape[1]
    half = left.shape[0] // 2
    copies = []
    for z, out, out_hbm in ((z_top, right, right_hbm), (z_low, upper, upper_hbm)):
        for r in range(2):
            here = pl.ds(r * half, half)
            out[here] = product(z.at[here], left, lower).astype(BF16)
            copies.append(
                pltpu.make_async_copy(out.at[here], out_hbm.at[here, pl.ds(0, width)], sem.at[len(copies)])
            )
            copies[-1].start()
    for copy in copies:
        copy.wait()


def last(z_top, z_low, left, lower, total):
    trace, width = left.shape
    out = jax.ShapeDtypeStruct((trace, total), BF16)
    return pl.pallas_call(
        last_kernel,
        out_shape=(out, out),
        in_specs=[VMEM] * 4,
        out_specs=(HBM, HBM),
        scratch_shapes=[
            pltpu.VMEM((trace, width), BF16),
            pltpu.VMEM((trace, width), BF16),
            pltpu.SemaphoreType.DMA((4,)),
        ],
        cost_estimate=cost(8 * trace * trace * width, 8 * trace * trace + 8 * trace * width),
        compiler_params=PARAMS,
        name="last",
    )(z_top, z_low, left, lower)


def plain_kernel(z_top, z_low, left, lower, right, upper):
    half = left.shape[0] // 2
    for z, out in ((z_top, right), (z_low, upper)):
        for r in range(2):
            here = pl.ds(r * half, half)
            out[here] = product(z.at[here], left, lower).astype(BF16)


def plain(z_top, z_low, left, lower):
    trace, width = left.shape
    out = jax.ShapeDtypeStruct((trace, width), BF16)
    return pl.pallas_call(
        plain_kernel,
        out_shape=(out, out),
        in_specs=[VMEM] * 4,
        out_specs=(VMEM, VMEM),
        cost_estimate=cost(8 * trace * trace * width, 8 * trace * trace + 8 * trace * width),
        compiler_params=PARAMS,
        name="plain",
    )(z_top, z_low, left, lower)


def beside(axis, pair, cross):
    place = lax.axis_index(axis)
    even = lax.rem(place, 2) == 0
    pair, cross = pair[...].astype(F32), cross[...].astype(F32)
    before = jnp.where(place == 0, 0.0, jnp.where(even, cross, pair))
    after = jnp.where(is_last(axis), 0.0, jnp.where(even, pair, cross))
    return before, after


def finish_kernel(cells_y, *refs):
    wavenum, right, upper, x_pair, x_cross, y_pair, y_cross = refs[:7]
    right_hbm, upper_hbm, residual_hbm, out, sem = refs[-5:]
    volumes = refs[7:-7]
    base = right_hbm.shape[1] - right.shape[1]
    copies = [
        pltpu.make_async_copy(right, right_hbm.at[:, pl.ds(base, right.shape[1])], sem.at[0]),
        pltpu.make_async_copy(upper, upper_hbm.at[:, pl.ds(base, upper.shape[1])], sem.at[1]),
    ]
    for copy in copies:
        copy.start()
    cells = volumes[0].shape[0]
    start = 0
    for volume in volumes:
        width = volume.shape[1]
        where = pl.ds(start, width)
        start += width
        before_x, after_x = beside("gx", x_pair.at[:, where], x_cross.at[:, where])
        before_y, after_y = beside("gy", y_pair.at[:, where], y_cross.at[:, where])
        place = lax.broadcasted_iota(jnp.int32, (cells_y, width), 0)
        for x in range(cells // cells_y):
            here = volume[pl.ds(x * cells_y, cells_y)]
            left = volume[pl.ds((x - 1) * cells_y, cells_y)] if x else before_x
            after = volume[pl.ds((x + 1) * cells_y, cells_y)] if (x + 1) * cells_y < cells else after_x
            below = jnp.where(place == 0, before_y[x : x + 1], pltpu.roll(here, 1, 0))
            above = jnp.where(place == cells_y - 1, after_y[x : x + 1], pltpu.roll(here, cells_y - 1, 0))
            scale = wavenum[pl.ds(x * cells_y, cells_y)][:, :1]
            out[x, :, where] = (after + left + above + below - 4.0 * here) + scale * here
        copies.append(
            pltpu.make_async_copy(out.at[:, :, where], residual_hbm.at[:, :, where], sem.at[len(copies)])
        )
        copies[-1].start()
    for copy in copies:
        copy.wait()


def finish(wavenum, right, upper, halos, volumes, outs, cells_y):
    cells = volumes[0].shape[0]
    total = outs[0].shape[1]
    whole = (cells // cells_y, cells_y, total)
    given = 3 + len(halos) + len(volumes)
    return pl.pallas_call(
        functools.partial(finish_kernel, cells_y),
        out_shape=tuple(jax.ShapeDtypeStruct(o.shape, o.dtype) for o in outs) + (jax.ShapeDtypeStruct(whole, F32),),
        in_specs=[VMEM] * given + [HBM] * 2,
        out_specs=(HBM,) * 3,
        scratch_shapes=[pltpu.VMEM(whole, F32), pltpu.SemaphoreType.DMA((2 + len(volumes),))],
        input_output_aliases={given: 0, given + 1: 1},
        cost_estimate=cost(10 * cells * total, 8 * cells * total),
        compiler_params=PARAMS,
        name="finish",
    )(wavenum, right, upper, *halos, *volumes, *outs)


def per_device(impedance, rebuild_map, left_trace, lower_trace, cell_kind, kind_wavenum):
    z = pltpu.with_memory_space_constraint(impedance[0, 0], pltpu.HBM)
    weights = rebuild_map[0, 0]
    left_all = pltpu.with_memory_space_constraint(left_trace[0, 0], pltpu.HBM)
    lower_all = pltpu.with_memory_space_constraint(lower_trace[0, 0], pltpu.HBM)
    sources = left_all.shape[1]
    width = sources // CHUNKS
    cells_x, cells_y = cell_kind.shape
    left_in, lower_in = [None] * CHUNKS, [None] * CHUNKS
    for step in range(STEPS - 1):
        for c in range(CHUNKS):
            if step == 0 and c == 0:
                right, z_top, left, lower = first_right(z, left_all, lower_all, 0, width)
            elif step == 0:
                right, left, lower = part_loading("gx", z_top, left_all, lower_all, c * width, width)
            else:
                left, lower = left_in[c], lower_in[c]
                right = part("gx", z_top, left, lower)
            left_in[c] = around(right, "gx")
            if step == 0 and c == 0:
                upper, z_low = first_upper(z, left, lower)
            else:
                upper = part("gy", z_low, left, lower)
            lower_in[c] = around(upper, "gy")

    wavenum = wavenum_of(kind_wavenum, cell_kind)
    volume_a = volume_of(weights, left_in[0], lower_in[0])
    outs = last(z_top, z_low, left_in[0], lower_in[0], sources)
    volume_a, wavenum, left_in[1], lower_in[1], *outs = lax.optimization_barrier(
        (volume_a, wavenum, left_in[1], lower_in[1], *outs)
    )
    volume_b, x_pair, x_cross, y_pair, y_cross = edges_of(weights, left_in[1], lower_in[1], volume_a, cells_y)
    x_cross = swapped(x_cross, "gx", 1)
    x_pair = swapped(x_pair, "gx", 0)
    y_cross = swapped(y_cross, "gy", 1)
    y_pair = swapped(y_pair, "gy", 0)
    halos = (x_pair, x_cross, y_pair, y_cross)
    right, upper = plain(z_top, z_low, left_in[1], lower_in[1])
    right_out, upper_out, residual = finish(
        wavenum, right, upper, halos, (volume_a, volume_b), outs, cells_y
    )
    return (right_out[None, None], upper_out[None, None], residual)


def solution(mesh):
    return jax.shard_map(
        per_device,
        mesh=mesh,
        in_specs=(
            P("gx", "gy", None, None),
            P("gx", "gy", None, None),
            P("gx", "gy", None, None),
            P("gx", "gy", None, None),
            P("gx", "gy"),
            P(),
        ),
        out_specs=(P("gx", "gy", None, None), P("gx", "gy", None, None), P("gx", "gy", None)),
        check_vma=False,
    )
```

```python
import functools

import jax
import jax.numpy as jnp
from jax import lax
from jax.experimental import pallas as pl
from jax.experimental.pallas import tpu as pltpu
from jax.sharding import PartitionSpec as P


STEPS = 4
CHUNKS = 2
F32 = jnp.float32
BF16 = jnp.bfloat16
VMEM = pl.BlockSpec(memory_space=pltpu.VMEM)
HBM = pl.BlockSpec(memory_space=pltpu.HBM)


def around(block, axis):
    count = lax.axis_size(axis)
    return lax.ppermute(block, axis, [(i, (i + 1) % count) for i in range(count)])


def onward(block, axis):
    count = lax.axis_size(axis)
    return lax.ppermute(block, axis, [(i, i + 1) for i in range(count - 1)])


def swapped(block, axis, first):
    names = ("gx", "gy")
    along = names.index(axis)
    sizes = tuple(lax.axis_size(name) for name in names)
    pairs = []
    for place in range(sizes[0] * sizes[1]):
        where = [place // sizes[1], place % sizes[1]]
        mate = first + ((where[along] - first) ^ 1)
        if 0 <= mate < sizes[along]:
            where[along] = mate
        elif axis == "gy":
            where[along] = sizes[along] - 1 - where[along]
        else:
            where[1 - along] ^= 1
        pairs.append((place, where[0] * sizes[1] + where[1]))
    return lax.ppermute(block, names, pairs)


def is_last(axis):
    return lax.axis_index(axis) == lax.axis_size(axis) - 1


PARAMS = pltpu.CompilerParams(vmem_limit_bytes=6 * 2**20)


def cost(flops, moved):
    return pl.CostEstimate(flops=int(flops), bytes_accessed=int(moved), transcendentals=0)


def product(weights, left, lower):
    half = left.shape[0]
    return jnp.dot(weights[:, :half], left[...], preferred_element_type=F32) + jnp.dot(
        weights[:, half:], lower[...], preferred_element_type=F32
    )


def first_right_kernel(base, width, z_hbm, left_hbm, lower_hbm, out, z_top, left, lower, sem):
    rows = z_top.shape[0]
    block = rows // 2
    loads = [
        pltpu.make_async_copy(left_hbm.at[:, pl.ds(base, width)], left, sem.at[0]),
        pltpu.make_async_copy(lower_hbm.at[:, pl.ds(base, width)], lower, sem.at[1]),
    ]
    parts = [
        pltpu.make_async_copy(z_hbm.at[pl.ds(r * block, block)], z_top.at[pl.ds(r * block, block)], sem.at[2 + r])
        for r in range(2)
    ]
    for copy in loads + parts:
        copy.start()
    for copy in loads:
        copy.wait()
    at_end = is_last("gx")
    for r in range(2):
        parts[r].wait()
        here = pl.ds(r * block, block)
        out[here] = jnp.where(at_end, 0.0, product(z_top.at[here], left, lower)).astype(BF16)


def first_right(z, left, lower, base, width):
    trace = left.shape[0]
    vmem = lambda *shape: jax.ShapeDtypeStruct(shape, BF16)
    return pl.pallas_call(
        functools.partial(first_right_kernel, base, width),
        out_shape=(vmem(trace, width), vmem(trace, 2 * trace), vmem(trace, width), vmem(trace, width)),
        in_specs=[HBM, HBM, HBM],
        out_specs=(VMEM,) * 4,
        scratch_shapes=[pltpu.SemaphoreType.DMA((4,))],
        cost_estimate=cost(4 * trace * trace * width, 4 * trace * trace + 6 * trace * width),
        compiler_params=PARAMS,
        name="first_right",
    )(z, left, lower)


def first_upper_kernel(z_hbm, left, lower, out, z_low, sem):
    rows = z_low.shape[0]
    block = rows // 2
    parts = [
        pltpu.make_async_copy(z_hbm.at[pl.ds(rows + r * block, block)], z_low.at[pl.ds(r * block, block)], sem.at[r])
        for r in range(2)
    ]
    for copy in parts:
        copy.start()
    at_end = is_last("gy")
    for r in range(2):
        parts[r].wait()
        here = pl.ds(r * block, block)
        out[here] = jnp.where(at_end, 0.0, product(z_low.at[here], left, lower)).astype(BF16)


def first_upper(z, left, lower):
    trace, width = left.shape
    vmem = lambda *shape: jax.ShapeDtypeStruct(shape, BF16)
    return pl.pallas_call(
        first_upper_kernel,
        out_shape=(vmem(trace, width), vmem(trace, 2 * trace)),
        in_specs=[HBM, VMEM, VMEM],
        out_specs=(VMEM,) * 2,
        scratch_shapes=[pltpu.SemaphoreType.DMA((2,))],
        cost_estimate=cost(4 * trace * trace * width, 4 * trace * trace + 6 * trace * width),
        compiler_params=PARAMS,
        name="first_upper",
    )(z, left, lower)


def part_kernel(axis, z, left, lower, out):
    half = left.shape[0] // 2
    at_end = is_last(axis)
    for r in range(2):
        here = pl.ds(r * half, half)
        out[here] = jnp.where(at_end, 0.0, product(z.at[here], left, lower)).astype(BF16)


def part(axis, z, left, lower):
    trace, width = left.shape
    return pl.pallas_call(
        functools.partial(part_kernel, axis),
        out_shape=jax.ShapeDtypeStruct((trace, width), BF16),
        in_specs=[VMEM] * 3,
        out_specs=VMEM,
        cost_estimate=cost(4 * trace * trace * width, 4 * trace * trace + 6 * trace * width),
        compiler_params=PARAMS,
        name="part",
    )(z, left, lower)


def part_loading_kernel(axis, base, z, left_hbm, lower_hbm, out, left, lower, sem):
    width = left.shape[1]
    loads = [
        pltpu.make_async_copy(left_hbm.at[:, pl.ds(base, width)], left, sem.at[0]),
        pltpu.make_async_copy(lower_hbm.at[:, pl.ds(base, width)], lower, sem.at[1]),
    ]
    for copy in loads:
        copy.start()
    for copy in loads:
        copy.wait()
    part_kernel(axis, z, left, lower, out)


def part_loading(axis, z, left, lower, base, width):
    trace = left.shape[0]
    block = jax.ShapeDtypeStruct((trace, width), BF16)
    return pl.pallas_call(
        functools.partial(part_loading_kernel, axis, base),
        out_shape=(block,) * 3,
        in_specs=[VMEM, HBM, HBM],
        out_specs=(VMEM,) * 3,
        scratch_shapes=[pltpu.SemaphoreType.DMA((2,))],
        cost_estimate=cost(4 * trace * trace * width, 4 * trace * trace + 6 * trace * width),
        compiler_params=PARAMS,
        name="part_loading",
    )(z, left, lower)


def wavenum_kernel(table, kinds, out):
    cells_x, cells_y = kinds.shape
    kind = kinds[...]
    value = jnp.zeros(kind.shape, F32)
    for k in range(table.shape[0]):
        value = jnp.where(kind == k, table[k], value)
    shape = (cells_y, cells_y)
    diagonal = lax.broadcasted_iota(jnp.int32, shape, 0) == lax.broadcasted_iota(jnp.int32, shape, 1)
    for x in range(cells_x):
        column = jnp.sum(jnp.where(diagonal, value[x : x + 1], 0.0), axis=1, keepdims=True)
        out[pl.ds(x * cells_y, cells_y)] = jnp.broadcast_to(column, (cells_y, out.shape[1]))


def wavenum_of(table, kinds):
    return pl.pallas_call(
        wavenum_kernel,
        out_shape=jax.ShapeDtypeStruct((kinds.size, 128), F32),
        in_specs=[pl.BlockSpec(memory_space=pltpu.SMEM), VMEM],
        out_specs=VMEM,
        compiler_params=PARAMS,
        name="wavenum",
    )(table, kinds)


def volume_kernel(weights, left, lower, volume):
    volume[...] = product(weights, left, lower)


def volume_of(weights, left, lower):
    width = left.shape[1]
    return pl.pallas_call(
        volume_kernel,
        out_shape=jax.ShapeDtypeStruct((weights.shape[0], width), F32),
        in_specs=[VMEM] * 3,
        out_specs=VMEM,
        cost_estimate=cost(2 * weights.size * width, 2 * weights.size + 4 * weights.shape[1] * width),
        compiler_params=PARAMS,
        name="volume",
    )(weights, left, lower)


def edges_kernel(cells_y, weights, left, lower, done, volume, x_pair, x_cross, y_pair, y_cross):
    cells = weights.shape[0]
    old = done.shape[1]
    volume[...] = product(weights, left, lower)
    even_x = lax.rem(lax.axis_index("gx"), 2) == 0
    even_y = lax.rem(lax.axis_index("gy"), 2) == 0
    for where, block in ((pl.ds(0, old), done), (pl.ds(old, volume.shape[1]), volume)):
        first = block[pl.ds(0, cells_y)]
        last = block[pl.ds(cells - cells_y, cells_y)]
        x_pair[:, where] = jnp.where(even_x, last, first).astype(BF16)
        x_cross[:, where] = jnp.where(even_x, first, last).astype(BF16)
        first = jnp.concatenate([block[pl.ds(x, 1)] for x in range(0, cells, cells_y)], axis=0)
        last = jnp.concatenate([block[pl.ds(x + cells_y - 1, 1)] for x in range(0, cells, cells_y)], axis=0)
        y_pair[:, where] = jnp.where(even_y, last, first).astype(BF16)
        y_cross[:, where] = jnp.where(even_y, first, last).astype(BF16)


def edges_of(weights, left, lower, done, cells_y):
    cells = weights.shape[0]
    width = left.shape[1]
    total = width + done.shape[1]
    line = lambda n: jax.ShapeDtypeStruct((n, total), BF16)
    return pl.pallas_call(
        functools.partial(edges_kernel, cells_y),
        out_shape=(
            jax.ShapeDtypeStruct((cells, width), F32),
            line(cells_y),
            line(cells_y),
            line(cells // cells_y),
            line(cells // cells_y),
        ),
        in_specs=[VMEM] * 4,
        out_specs=(VMEM,) * 5,
        cost_estimate=cost(2 * weights.size * width, 2 * weights.size + 4 * weights.shape[1] * width),
        compiler_params=PARAMS,
        name="edges",
    )(weights, left, lower, done)


def last_kernel(z_top, z_low, left, lower, right_hbm, upper_hbm, right, upper, sem):
    width = left.shape[1]
    half = left.shape[0] // 2
    copies = []
    for z, out, out_hbm in ((z_top, right, right_hbm), (z_low, upper, upper_hbm)):
        for r in range(2):
            here = pl.ds(r * half, half)
            out[here] = product(z.at[here], left, lower).astype(BF16)
            copies.append(
                pltpu.make_async_copy(out.at[here], out_hbm.at[here, pl.ds(0, width)], sem.at[len(copies)])
            )
            copies[-1].start()
    for copy in copies:
        copy.wait()


def last(z_top, z_low, left, lower, total):
    trace, width = left.shape
    out = jax.ShapeDtypeStruct((trace, total), BF16)
    return pl.pallas_call(
        last_kernel,
        out_shape=(out, out),
        in_specs=[VMEM] * 4,
        out_specs=(HBM, HBM),
        scratch_shapes=[
            pltpu.VMEM((trace, width), BF16),
            pltpu.VMEM((trace, width), BF16),
            pltpu.SemaphoreType.DMA((4,)),
        ],
        cost_estimate=cost(8 * trace * trace * width, 8 * trace * trace + 8 * trace * width),
        compiler_params=PARAMS,
        name="last",
    )(z_top, z_low, left, lower)


def plain_kernel(z_top, z_low, left, lower, right, upper):
    half = left.shape[0] // 2
    for z, out in ((z_top, right), (z_low, upper)):
        for r in range(2):
            here = pl.ds(r * half, half)
            out[here] = product(z.at[here], left, lower).astype(BF16)


def plain(z_top, z_low, left, lower):
    trace, width = left.shape
    out = jax.ShapeDtypeStruct((trace, width), BF16)
    return pl.pallas_call(
        plain_kernel,
        out_shape=(out, out),
        in_specs=[VMEM] * 4,
        out_specs=(VMEM, VMEM),
        cost_estimate=cost(8 * trace * trace * width, 8 * trace * trace + 8 * trace * width),
        compiler_params=PARAMS,
        name="plain",
    )(z_top, z_low, left, lower)


def beside(axis, pair, cross):
    place = lax.axis_index(axis)
    even = lax.rem(place, 2) == 0
    pair, cross = pair[...].astype(F32), cross[...].astype(F32)
    before = jnp.where(place == 0, 0.0, jnp.where(even, cross, pair))
    after = jnp.where(is_last(axis), 0.0, jnp.where(even, pair, cross))
    return before, after


def finish_kernel(cells_y, *refs):
    wavenum, right, upper, x_pair, x_cross, y_pair, y_cross = refs[:7]
    right_hbm, upper_hbm, residual_hbm, out, sem = refs[-5:]
    volumes = refs[7:-7]
    base = right_hbm.shape[1] - right.shape[1]
    copies = [
        pltpu.make_async_copy(right, right_hbm.at[:, pl.ds(base, right.shape[1])], sem.at[0]),
        pltpu.make_async_copy(upper, upper_hbm.at[:, pl.ds(base, upper.shape[1])], sem.at[1]),
    ]
    for copy in copies:
        copy.start()
    cells = volumes[0].shape[0]
    start = 0
    for volume in volumes:
        width = volume.shape[1]
        where = pl.ds(start, width)
        start += width
        before_x, after_x = beside("gx", x_pair.at[:, where], x_cross.at[:, where])
        before_y, after_y = beside("gy", y_pair.at[:, where], y_cross.at[:, where])
        place = lax.broadcasted_iota(jnp.int32, (cells_y, width), 0)
        for x in range(cells // cells_y):
            here = volume[pl.ds(x * cells_y, cells_y)]
            left = volume[pl.ds((x - 1) * cells_y, cells_y)] if x else before_x
            after = volume[pl.ds((x + 1) * cells_y, cells_y)] if (x + 1) * cells_y < cells else after_x
            below = jnp.where(place == 0, before_y[x : x + 1], pltpu.roll(here, 1, 0))
            above = jnp.where(place == cells_y - 1, after_y[x : x + 1], pltpu.roll(here, cells_y - 1, 0))
            scale = wavenum[pl.ds(x * cells_y, cells_y)][:, :1]
            out[x, :, where] = (after + left + above + below - 4.0 * here) + scale * here
        copies.append(
            pltpu.make_async_copy(out.at[:, :, where], residual_hbm.at[:, :, where], sem.at[len(copies)])
        )
        copies[-1].start()
    for copy in copies:
        copy.wait()


def finish(wavenum, right, upper, halos, volumes, outs, cells_y):
    cells = volumes[0].shape[0]
    total = outs[0].shape[1]
    whole = (cells // cells_y, cells_y, total)
    given = 3 + len(halos) + len(volumes)
    return pl.pallas_call(
        functools.partial(finish_kernel, cells_y),
        out_shape=tuple(jax.ShapeDtypeStruct(o.shape, o.dtype) for o in outs) + (jax.ShapeDtypeStruct(whole, F32),),
        in_specs=[VMEM] * given + [HBM] * 2,
        out_specs=(HBM,) * 3,
        scratch_shapes=[pltpu.VMEM(whole, F32), pltpu.SemaphoreType.DMA((2 + len(volumes),))],
        input_output_aliases={given: 0, given + 1: 1},
        cost_estimate=cost(10 * cells * total, 8 * cells * total),
        compiler_params=PARAMS,
        name="finish",
    )(wavenum, right, upper, *halos, *volumes, *outs)


def per_device(impedance, rebuild_map, left_trace, lower_trace, cell_kind, kind_wavenum):
    z = pltpu.with_memory_space_constraint(impedance[0, 0], pltpu.HBM)
    weights = rebuild_map[0, 0]
    left_all = pltpu.with_memory_space_constraint(left_trace[0, 0], pltpu.HBM)
    lower_all = pltpu.with_memory_space_constraint(lower_trace[0, 0], pltpu.HBM)
    sources = left_all.shape[1]
    width = sources // CHUNKS
    _, cells_y = cell_kind.shape
    left_in, lower_in = [None] * CHUNKS, [None] * CHUNKS
    for step in range(STEPS - 1):
        for c in range(CHUNKS):
            if step == 0 and c == 0:
                right, z_top, left, lower = first_right(z, left_all, lower_all, 0, width)
            elif step == 0:
                right, left, lower = part_loading("gx", z_top, left_all, lower_all, c * width, width)
            else:
                left, lower = left_in[c], lower_in[c]
                right = part("gx", z_top, left, lower)
            final = step == STEPS - 2 and c == CHUNKS - 1
            left_in[c] = onward(right, "gx") if final else around(right, "gx")
            if step == 0 and c == 0:
                upper, z_low = first_upper(z, left, lower)
            else:
                upper = part("gy", z_low, left, lower)
            lower_in[c] = around(upper, "gy")

    wavenum = wavenum_of(kind_wavenum, cell_kind)
    volume_a = volume_of(weights, left_in[0], lower_in[0])
    outs = last(z_top, z_low, left_in[0], lower_in[0], sources)
    volume_a, wavenum, left_in[1], lower_in[1], *outs = lax.optimization_barrier(
        (volume_a, wavenum, left_in[1], lower_in[1], *outs)
    )
    volume_b, x_pair, x_cross, y_pair, y_cross = edges_of(weights, left_in[1], lower_in[1], volume_a, cells_y)
    x_pair = swapped(x_pair, "gx", 0)
    x_cross = swapped(x_cross, "gx", 1)
    y_cross = swapped(y_cross, "gy", 1)
    y_pair = swapped(y_pair, "gy", 0)
    halos = (x_pair, x_cross, y_pair, y_cross)
    right, upper = plain(z_top, z_low, left_in[1], lower_in[1])
    right_out, upper_out, residual = finish(
        wavenum, right, upper, halos, (volume_a, volume_b), outs, cells_y
    )
    return (right_out[None, None], upper_out[None, None], residual)


def solution(mesh):
    return jax.shard_map(
        per_device,
        mesh=mesh,
        in_specs=(
            P("gx", "gy", None, None),
            P("gx", "gy", None, None),
            P("gx", "gy", None, None),
            P("gx", "gy", None, None),
            P("gx", "gy"),
            P(),
        ),
        out_specs=(P("gx", "gy", None, None), P("gx", "gy", None, None), P("gx", "gy", None)),
        check_vma=False,
    )
```

```python
import functools

import jax
import jax.numpy as jnp
from jax import lax
from jax.experimental import pallas as pl
from jax.experimental.pallas import tpu as pltpu
from jax.sharding import PartitionSpec as P


STEPS = 4
CHUNKS = 2
F32 = jnp.float32
BF16 = jnp.bfloat16
VMEM = pl.BlockSpec(memory_space=pltpu.VMEM)
HBM = pl.BlockSpec(memory_space=pltpu.HBM)


def around(block, axis):
    count = lax.axis_size(axis)
    return lax.ppermute(block, axis, [(i, (i + 1) % count) for i in range(count)])


def onward(block, axis):
    count = lax.axis_size(axis)
    return lax.ppermute(block, axis, [(i, i + 1) for i in range(count - 1)])


def swapped(block, axis, first):
    names = ("gx", "gy")
    along = names.index(axis)
    sizes = tuple(lax.axis_size(name) for name in names)
    pairs = []
    for place in range(sizes[0] * sizes[1]):
        where = [place // sizes[1], place % sizes[1]]
        mate = first + ((where[along] - first) ^ 1)
        if 0 <= mate < sizes[along]:
            where[along] = mate
        elif axis == "gy":
            where[along] = sizes[along] - 1 - where[along]
        else:
            where[1 - along] ^= 1
        pairs.append((place, where[0] * sizes[1] + where[1]))
    return lax.ppermute(block, names, pairs)


def is_last(axis):
    return lax.axis_index(axis) == lax.axis_size(axis) - 1


PARAMS = pltpu.CompilerParams(vmem_limit_bytes=6 * 2**20)


def cost(flops, moved):
    return pl.CostEstimate(flops=int(flops), bytes_accessed=int(moved), transcendentals=0)


def product(weights, left, lower):
    total, start = None, 0
    for piece in (*left, lower):
        rows = piece.shape[0]
        share = jnp.dot(weights[:, start : start + rows], piece[...], preferred_element_type=F32)
        total = share if total is None else total + share
        start += rows
    return total


def first_right_kernel(base, width, z_hbm, left_hbm, lower_hbm, out, z_top, left, lower, sem):
    rows = z_top.shape[0]
    block = rows // 2
    loads = [
        pltpu.make_async_copy(left_hbm.at[:, pl.ds(base, width)], left, sem.at[0]),
        pltpu.make_async_copy(lower_hbm.at[:, pl.ds(base, width)], lower, sem.at[1]),
    ]
    parts = [
        pltpu.make_async_copy(z_hbm.at[pl.ds(r * block, block)], z_top.at[pl.ds(r * block, block)], sem.at[2 + r])
        for r in range(2)
    ]
    for copy in loads + parts:
        copy.start()
    for copy in loads:
        copy.wait()
    at_end = is_last("gx")
    for r in range(2):
        parts[r].wait()
        here = pl.ds(r * block, block)
        out[here] = jnp.where(at_end, 0.0, product(z_top.at[here], [left], lower)).astype(BF16)


def first_right(z, left, lower, base, width):
    trace = left.shape[0]
    vmem = lambda *shape: jax.ShapeDtypeStruct(shape, BF16)
    return pl.pallas_call(
        functools.partial(first_right_kernel, base, width),
        out_shape=(vmem(trace, width), vmem(trace, 2 * trace), vmem(trace, width), vmem(trace, width)),
        in_specs=[HBM, HBM, HBM],
        out_specs=(VMEM,) * 4,
        scratch_shapes=[pltpu.SemaphoreType.DMA((4,))],
        cost_estimate=cost(4 * trace * trace * width, 4 * trace * trace + 6 * trace * width),
        compiler_params=PARAMS,
        name="first_right",
    )(z, left, lower)


def first_upper_kernel(z_hbm, left, lower, out, z_low, sem):
    rows = z_low.shape[0]
    block = rows // 2
    parts = [
        pltpu.make_async_copy(z_hbm.at[pl.ds(rows + r * block, block)], z_low.at[pl.ds(r * block, block)], sem.at[r])
        for r in range(2)
    ]
    for copy in parts:
        copy.start()
    at_end = is_last("gy")
    for r in range(2):
        parts[r].wait()
        here = pl.ds(r * block, block)
        out[here] = jnp.where(at_end, 0.0, product(z_low.at[here], [left], lower)).astype(BF16)


def first_upper(z, left, lower):
    trace, width = left.shape
    vmem = lambda *shape: jax.ShapeDtypeStruct(shape, BF16)
    return pl.pallas_call(
        first_upper_kernel,
        out_shape=(vmem(trace, width), vmem(trace, 2 * trace)),
        in_specs=[HBM, VMEM, VMEM],
        out_specs=(VMEM,) * 2,
        scratch_shapes=[pltpu.SemaphoreType.DMA((2,))],
        cost_estimate=cost(4 * trace * trace * width, 4 * trace * trace + 6 * trace * width),
        compiler_params=PARAMS,
        name="first_upper",
    )(z, left, lower)


def part_kernel(axis, z, left, lower, out):
    half = left.shape[0] // 2
    at_end = is_last(axis)
    for r in range(2):
        here = pl.ds(r * half, half)
        out[here] = jnp.where(at_end, 0.0, product(z.at[here], [left], lower)).astype(BF16)


def part(axis, z, left, lower):
    trace, width = left.shape
    return pl.pallas_call(
        functools.partial(part_kernel, axis),
        out_shape=jax.ShapeDtypeStruct((trace, width), BF16),
        in_specs=[VMEM] * 3,
        out_specs=VMEM,
        cost_estimate=cost(4 * trace * trace * width, 4 * trace * trace + 6 * trace * width),
        compiler_params=PARAMS,
        name="part",
    )(z, left, lower)


def part_loading_kernel(axis, base, z, left_hbm, lower_hbm, out, left, lower, sem):
    width = left.shape[1]
    loads = [
        pltpu.make_async_copy(left_hbm.at[:, pl.ds(base, width)], left, sem.at[0]),
        pltpu.make_async_copy(lower_hbm.at[:, pl.ds(base, width)], lower, sem.at[1]),
    ]
    for copy in loads:
        copy.start()
    for copy in loads:
        copy.wait()
    part_kernel(axis, z, left, lower, out)


def part_loading(axis, z, left, lower, base, width):
    trace = left.shape[0]
    block = jax.ShapeDtypeStruct((trace, width), BF16)
    return pl.pallas_call(
        functools.partial(part_loading_kernel, axis, base),
        out_shape=(block,) * 3,
        in_specs=[VMEM, HBM, HBM],
        out_specs=(VMEM,) * 3,
        scratch_shapes=[pltpu.SemaphoreType.DMA((2,))],
        cost_estimate=cost(4 * trace * trace * width, 4 * trace * trace + 6 * trace * width),
        compiler_params=PARAMS,
        name="part_loading",
    )(z, left, lower)


def wavenum_kernel(table, kinds, out):
    cells_x, cells_y = kinds.shape
    kind = kinds[...]
    value = jnp.zeros(kind.shape, F32)
    for k in range(table.shape[0]):
        value = jnp.where(kind == k, table[k], value)
    shape = (cells_y, cells_y)
    diagonal = lax.broadcasted_iota(jnp.int32, shape, 0) == lax.broadcasted_iota(jnp.int32, shape, 1)
    for x in range(cells_x):
        column = jnp.sum(jnp.where(diagonal, value[x : x + 1], 0.0), axis=1, keepdims=True)
        out[pl.ds(x * cells_y, cells_y)] = jnp.broadcast_to(column, (cells_y, out.shape[1]))


def wavenum_of(table, kinds):
    return pl.pallas_call(
        wavenum_kernel,
        out_shape=jax.ShapeDtypeStruct((kinds.size, 128), F32),
        in_specs=[pl.BlockSpec(memory_space=pltpu.SMEM), VMEM],
        out_specs=VMEM,
        compiler_params=PARAMS,
        name="wavenum",
    )(table, kinds)


def volume_kernel(weights, left, lower, volume):
    volume[...] = product(weights, [left], lower)


def volume_of(weights, left, lower):
    width = left.shape[1]
    return pl.pallas_call(
        volume_kernel,
        out_shape=jax.ShapeDtypeStruct((weights.shape[0], width), F32),
        in_specs=[VMEM] * 3,
        out_specs=VMEM,
        cost_estimate=cost(2 * weights.size * width, 2 * weights.size + 4 * weights.shape[1] * width),
        compiler_params=PARAMS,
        name="volume",
    )(weights, left, lower)


def edges_kernel(cells_y, weights, lower, done, *refs):
    left = refs[:-5]
    volume, x_pair, x_cross, y_pair, y_cross = refs[-5:]
    cells = weights.shape[0]
    old = done.shape[1]
    volume[...] = product(weights, left, lower)
    even_x = lax.rem(lax.axis_index("gx"), 2) == 0
    even_y = lax.rem(lax.axis_index("gy"), 2) == 0
    for where, block in ((pl.ds(0, old), done), (pl.ds(old, volume.shape[1]), volume)):
        first = block[pl.ds(0, cells_y)]
        last = block[pl.ds(cells - cells_y, cells_y)]
        x_pair[:, where] = jnp.where(even_x, last, first).astype(BF16)
        x_cross[:, where] = jnp.where(even_x, first, last).astype(BF16)
        first = jnp.concatenate([block[pl.ds(x, 1)] for x in range(0, cells, cells_y)], axis=0)
        last = jnp.concatenate([block[pl.ds(x + cells_y - 1, 1)] for x in range(0, cells, cells_y)], axis=0)
        y_pair[:, where] = jnp.where(even_y, last, first).astype(BF16)
        y_cross[:, where] = jnp.where(even_y, first, last).astype(BF16)


def edges_of(weights, left, lower, done, cells_y):
    cells = weights.shape[0]
    width = lower.shape[1]
    total = width + done.shape[1]
    line = lambda n: jax.ShapeDtypeStruct((n, total), BF16)
    return pl.pallas_call(
        functools.partial(edges_kernel, cells_y),
        out_shape=(
            jax.ShapeDtypeStruct((cells, width), F32),
            line(cells_y),
            line(cells_y),
            line(cells // cells_y),
            line(cells // cells_y),
        ),
        in_specs=[VMEM] * (3 + len(left)),
        out_specs=(VMEM,) * 5,
        cost_estimate=cost(2 * weights.size * width, 2 * weights.size + 4 * weights.shape[1] * width),
        compiler_params=PARAMS,
        name="edges",
    )(weights, lower, done, *left)


def last_kernel(z_top, z_low, left, lower, right_hbm, upper_hbm, right, upper, sem):
    width = left.shape[1]
    half = left.shape[0] // 2
    copies = []
    for z, out, out_hbm in ((z_top, right, right_hbm), (z_low, upper, upper_hbm)):
        for r in range(2):
            here = pl.ds(r * half, half)
            out[here] = product(z.at[here], [left], lower).astype(BF16)
            copies.append(
                pltpu.make_async_copy(out.at[here], out_hbm.at[here, pl.ds(0, width)], sem.at[len(copies)])
            )
            copies[-1].start()
    for copy in copies:
        copy.wait()


def last(z_top, z_low, left, lower, total):
    trace, width = left.shape
    out = jax.ShapeDtypeStruct((trace, total), BF16)
    return pl.pallas_call(
        last_kernel,
        out_shape=(out, out),
        in_specs=[VMEM] * 4,
        out_specs=(HBM, HBM),
        scratch_shapes=[
            pltpu.VMEM((trace, width), BF16),
            pltpu.VMEM((trace, width), BF16),
            pltpu.SemaphoreType.DMA((4,)),
        ],
        cost_estimate=cost(8 * trace * trace * width, 8 * trace * trace + 8 * trace * width),
        compiler_params=PARAMS,
        name="last",
    )(z_top, z_low, left, lower)


def plain_kernel(z_top, z_low, lower, wavenum, first, second, *refs):
    right_hbm, upper_hbm, inner, right, upper, sem = refs[-6:]
    left = refs[:-8]
    half, width = right.shape[0] // 2, right.shape[1]
    base = right_hbm.shape[1] - width
    copies = []
    for z, out, out_hbm in ((z_top, right, right_hbm), (z_low, upper, upper_hbm)):
        for r in range(2):
            here = pl.ds(r * half, half)
            out[here] = product(z.at[here], left, lower).astype(BF16)
            copies.append(
                pltpu.make_async_copy(out.at[here], out_hbm.at[here, pl.ds(base, width)], sem.at[len(copies)])
            )
            copies[-1].start()
    cells_x, cells_y = inner.shape[:2]
    start = 0
    for volume in (first, second):
        where = pl.ds(start, volume.shape[1])
        start += volume.shape[1]
        place = lax.broadcasted_iota(jnp.int32, (cells_y, volume.shape[1]), 0)
        for x in range(cells_x):
            row = lambda k: volume[pl.ds(k * cells_y, cells_y)]
            here = row(x)
            around_it = jnp.where(place == 0, 0.0, pltpu.roll(here, 1, 0)) + jnp.where(
                place == cells_y - 1, 0.0, pltpu.roll(here, cells_y - 1, 0)
            )
            if x:
                around_it = around_it + row(x - 1)
            if x + 1 < cells_x:
                around_it = around_it + row(x + 1)
            scale = wavenum[pl.ds(x * cells_y, cells_y)][:, :1]
            inner[x, :, where] = around_it - 4.0 * here + scale * here
    for copy in copies:
        copy.wait()


def plain(z_top, z_low, left, lower, wavenum, volumes, outs, cells_y):
    trace, width = lower.shape
    cells = volumes[0].shape[0]
    total = outs[0].shape[1]
    given = 6 + len(left)
    return pl.pallas_call(
        plain_kernel,
        out_shape=tuple(jax.ShapeDtypeStruct(o.shape, o.dtype) for o in outs)
        + (jax.ShapeDtypeStruct((cells // cells_y, cells_y, total), F32),),
        in_specs=[VMEM] * given + [HBM] * 2,
        out_specs=(HBM, HBM, VMEM),
        scratch_shapes=[
            pltpu.VMEM((trace, width), BF16),
            pltpu.VMEM((trace, width), BF16),
            pltpu.SemaphoreType.DMA((4,)),
        ],
        input_output_aliases={given: 0, given + 1: 1},
        cost_estimate=cost(8 * trace * trace * width, 8 * trace * trace + 8 * trace * width),
        compiler_params=PARAMS,
        name="plain",
    )(z_top, z_low, lower, wavenum, *volumes, *left, *outs)


def beside(axis, pair, cross):
    place = lax.axis_index(axis)
    even = lax.rem(place, 2) == 0
    pair, cross = pair[...].astype(F32), cross[...].astype(F32)
    before = jnp.where(place == 0, 0.0, jnp.where(even, cross, pair))
    after = jnp.where(is_last(axis), 0.0, jnp.where(even, pair, cross))
    return before, after


def finish_kernel(inner, x_pair, x_cross, y_pair, y_cross, residual_hbm, out, sem):
    cells_x, cells_y, total = inner.shape
    groups = sem.shape[0]
    deep = cells_x // groups
    before_x, after_x = beside("gx", x_pair, x_cross)
    before_y, after_y = beside("gy", y_pair, y_cross)
    place = lax.broadcasted_iota(jnp.int32, (cells_y, total), 0)
    copies = []
    for group in range(groups):
        for x in range(group * deep, (group + 1) * deep):
            value = inner[x]
            value = value + jnp.where(
                place == 0, before_y[x : x + 1], jnp.where(place == cells_y - 1, after_y[x : x + 1], 0.0)
            )
            if x == 0:
                value = value + before_x
            if x == cells_x - 1:
                value = value + after_x
            out[x] = value
        here = pl.ds(group * deep, deep)
        copies.append(pltpu.make_async_copy(out.at[here], residual_hbm.at[here], sem.at[group]))
        copies[-1].start()
    for copy in copies:
        copy.wait()


def finish(inner, halos):
    groups = 2 if inner.shape[0] % 2 == 0 else 1
    return pl.pallas_call(
        finish_kernel,
        out_shape=jax.ShapeDtypeStruct(inner.shape, F32),
        in_specs=[VMEM] * (1 + len(halos)),
        out_specs=HBM,
        scratch_shapes=[pltpu.VMEM(inner.shape, F32), pltpu.SemaphoreType.DMA((groups,))],
        cost_estimate=cost(4 * inner.size, 8 * inner.size),
        compiler_params=PARAMS,
        name="finish",
    )(inner, *halos)


def per_device(impedance, rebuild_map, left_trace, lower_trace, cell_kind, kind_wavenum):
    z = pltpu.with_memory_space_constraint(impedance[0, 0], pltpu.HBM)
    weights = rebuild_map[0, 0]
    left_all = pltpu.with_memory_space_constraint(left_trace[0, 0], pltpu.HBM)
    lower_all = pltpu.with_memory_space_constraint(lower_trace[0, 0], pltpu.HBM)
    sources = left_all.shape[1]
    width = sources // CHUNKS
    _, cells_y = cell_kind.shape
    left_in, lower_in = [None] * CHUNKS, [None] * CHUNKS
    for step in range(STEPS - 1):
        for c in range(CHUNKS):
            if step == 0 and c == 0:
                right, z_top, left, lower = first_right(z, left_all, lower_all, 0, width)
            elif step == 0:
                right, left, lower = part_loading("gx", z_top, left_all, lower_all, c * width, width)
            else:
                left, lower = left_in[c], lower_in[c]
                right = part("gx", z_top, left, lower)
            final = step == STEPS - 2 and c == CHUNKS - 1
            left_in[c] = onward(right, "gx") if final else around(right, "gx")
            if step == 0 and c == 0:
                upper, z_low = first_upper(z, left, lower)
            else:
                upper = part("gy", z_low, left, lower)
            lower_in[c] = around(upper, "gy")

    left_in[-1] = (left_in[-1],)
    wavenum = wavenum_of(kind_wavenum, cell_kind)
    volume_a = volume_of(weights, left_in[0], lower_in[0])
    outs = last(z_top, z_low, left_in[0], lower_in[0], sources)
    volume_a, wavenum, left, lower, *outs = lax.optimization_barrier(
        (volume_a, wavenum, left_in[1], lower_in[1], *outs)
    )
    volume_b, x_pair, x_cross, y_pair, y_cross = edges_of(weights, left, lower, volume_a, cells_y)
    x_pair = swapped(x_pair, "gx", 0)
    x_cross = swapped(x_cross, "gx", 1)
    y_cross = swapped(y_cross, "gy", 1)
    y_pair = swapped(y_pair, "gy", 0)
    halos = (x_pair, x_cross, y_pair, y_cross)
    right_out, upper_out, inner = plain(
        z_top, z_low, left, lower, wavenum, (volume_a, volume_b), outs, cells_y
    )
    residual = finish(inner, halos)
    return (right_out[None, None], upper_out[None, None], residual)


def solution(mesh):
    return jax.shard_map(
        per_device,
        mesh=mesh,
        in_specs=(
            P("gx", "gy", None, None),
            P("gx", "gy", None, None),
            P("gx", "gy", None, None),
            P("gx", "gy", None, None),
            P("gx", "gy"),
            P(),
        ),
        out_specs=(P("gx", "gy", None, None), P("gx", "gy", None, None), P("gx", "gy", None)),
        check_vma=False,
    )
```

```python
import functools

import jax
import jax.numpy as jnp
from jax import lax
from jax.experimental import pallas as pl
from jax.experimental.pallas import tpu as pltpu
from jax.sharding import PartitionSpec as P


STEPS = 4
CHUNKS = 2
F32 = jnp.float32
BF16 = jnp.bfloat16
VMEM = pl.BlockSpec(memory_space=pltpu.VMEM)
HBM = pl.BlockSpec(memory_space=pltpu.HBM)


def around(block, axis):
    count = lax.axis_size(axis)
    return lax.ppermute(block, axis, [(i, (i + 1) % count) for i in range(count)])


def onward(block, axis):
    count = lax.axis_size(axis)
    return lax.ppermute(block, axis, [(i, i + 1) for i in range(count - 1)])


def swapped(block, axis, first):
    names = ("gx", "gy")
    along = names.index(axis)
    sizes = tuple(lax.axis_size(name) for name in names)
    pairs = []
    for place in range(sizes[0] * sizes[1]):
        where = [place // sizes[1], place % sizes[1]]
        mate = first + ((where[along] - first) ^ 1)
        if 0 <= mate < sizes[along]:
            where[along] = mate
        elif axis == "gy":
            where[along] = sizes[along] - 1 - where[along]
        else:
            where[1 - along] ^= 1
        pairs.append((place, where[0] * sizes[1] + where[1]))
    return lax.ppermute(block, names, pairs)


def is_last(axis):
    return lax.axis_index(axis) == lax.axis_size(axis) - 1


PARAMS = pltpu.CompilerParams(vmem_limit_bytes=6 * 2**20)
PACKED = pltpu.CompilerParams(vmem_limit_bytes=6 * 2**20)


def cost(flops, moved):
    return pl.CostEstimate(flops=int(flops), bytes_accessed=int(moved), transcendentals=0)


def product(weights, left, lower):
    total, start = None, 0
    for piece in (*left, lower):
        rows = piece.shape[0]
        share = jnp.dot(weights[:, start : start + rows], piece[...], preferred_element_type=F32)
        total = share if total is None else total + share
        start += rows
    return total


def first_right_kernel(base, width, z_hbm, left_hbm, lower_hbm, out, z_top, left, lower, sem):
    rows = z_top.shape[0]
    split = rows * 6 // 8
    blocks = (pl.ds(0, split), pl.ds(split, rows - split))
    loads = [
        pltpu.make_async_copy(left_hbm.at[:, pl.ds(base, width)], left, sem.at[0]),
        pltpu.make_async_copy(lower_hbm.at[:, pl.ds(base, width)], lower, sem.at[1]),
    ]
    parts = [pltpu.make_async_copy(z_hbm.at[here], z_top.at[here], sem.at[2 + r]) for r, here in enumerate(blocks)]
    for copy in loads + parts:
        copy.start()
    for copy in loads:
        copy.wait()
    at_end = is_last("gx")
    for copy, here in zip(parts, blocks):
        copy.wait()
        out[here] = jnp.where(at_end, 0.0, product(z_top.at[here], [left], lower)).astype(BF16)


def first_right(z, left, lower, base, width):
    trace = left.shape[0]
    vmem = lambda *shape: jax.ShapeDtypeStruct(shape, BF16)
    return pl.pallas_call(
        functools.partial(first_right_kernel, base, width),
        out_shape=(vmem(trace, width), vmem(trace, 2 * trace), vmem(trace, width), vmem(trace, width)),
        in_specs=[HBM, HBM, HBM],
        out_specs=(VMEM,) * 4,
        scratch_shapes=[pltpu.SemaphoreType.DMA((4,))],
        cost_estimate=cost(4 * trace * trace * width, 4 * trace * trace + 6 * trace * width),
        compiler_params=PARAMS,
        name="first_right",
    )(z, left, lower)


def first_upper_kernel(z_hbm, left, lower, out, z_low, sem):
    rows = z_low.shape[0]
    block = rows // 2
    parts = [
        pltpu.make_async_copy(z_hbm.at[pl.ds(rows + r * block, block)], z_low.at[pl.ds(r * block, block)], sem.at[r])
        for r in range(2)
    ]
    for copy in parts:
        copy.start()
    at_end = is_last("gy")
    for r in range(2):
        parts[r].wait()
        here = pl.ds(r * block, block)
        out[here] = jnp.where(at_end, 0.0, product(z_low.at[here], [left], lower)).astype(BF16)


def first_upper(z, left, lower):
    trace, width = left.shape
    vmem = lambda *shape: jax.ShapeDtypeStruct(shape, BF16)
    return pl.pallas_call(
        first_upper_kernel,
        out_shape=(vmem(trace, width), vmem(trace, 2 * trace)),
        in_specs=[HBM, VMEM, VMEM],
        out_specs=(VMEM,) * 2,
        scratch_shapes=[pltpu.SemaphoreType.DMA((2,))],
        cost_estimate=cost(4 * trace * trace * width, 4 * trace * trace + 6 * trace * width),
        compiler_params=PARAMS,
        name="first_upper",
    )(z, left, lower)


def part_kernel(axis, z, left, lower, out):
    half = left.shape[0] // 2
    at_end = is_last(axis)
    for r in range(2):
        here = pl.ds(r * half, half)
        out[here] = jnp.where(at_end, 0.0, product(z.at[here], [left], lower)).astype(BF16)


def part(axis, z, left, lower):
    trace, width = left.shape
    return pl.pallas_call(
        functools.partial(part_kernel, axis),
        out_shape=jax.ShapeDtypeStruct((trace, width), BF16),
        in_specs=[VMEM] * 3,
        out_specs=VMEM,
        cost_estimate=cost(4 * trace * trace * width, 4 * trace * trace + 6 * trace * width),
        compiler_params=PARAMS,
        name="part",
    )(z, left, lower)


def part_loading_kernel(axis, base, z, left_hbm, lower_hbm, out, left, lower, sem):
    width = left.shape[1]
    loads = [
        pltpu.make_async_copy(left_hbm.at[:, pl.ds(base, width)], left, sem.at[0]),
        pltpu.make_async_copy(lower_hbm.at[:, pl.ds(base, width)], lower, sem.at[1]),
    ]
    for copy in loads:
        copy.start()
    for copy in loads:
        copy.wait()
    part_kernel(axis, z, left, lower, out)


def part_loading(axis, z, left, lower, base, width):
    trace = left.shape[0]
    block = jax.ShapeDtypeStruct((trace, width), BF16)
    return pl.pallas_call(
        functools.partial(part_loading_kernel, axis, base),
        out_shape=(block,) * 3,
        in_specs=[VMEM, HBM, HBM],
        out_specs=(VMEM,) * 3,
        scratch_shapes=[pltpu.SemaphoreType.DMA((2,))],
        cost_estimate=cost(4 * trace * trace * width, 4 * trace * trace + 6 * trace * width),
        compiler_params=PARAMS,
        name="part_loading",
    )(z, left, lower)


def wavenum_kernel(table, kinds, out):
    cells_x, cells_y = kinds.shape
    kind = kinds[...]
    value = jnp.zeros(kind.shape, F32)
    for k in range(table.shape[0]):
        value = jnp.where(kind == k, table[k], value)
    shape = (cells_y, cells_y)
    diagonal = lax.broadcasted_iota(jnp.int32, shape, 0) == lax.broadcasted_iota(jnp.int32, shape, 1)
    for x in range(cells_x):
        column = jnp.sum(jnp.where(diagonal, value[x : x + 1], 0.0), axis=1, keepdims=True)
        out[pl.ds(x * cells_y, cells_y)] = jnp.broadcast_to(column, (cells_y, out.shape[1]))


def wavenum_of(table, kinds):
    return pl.pallas_call(
        wavenum_kernel,
        out_shape=jax.ShapeDtypeStruct((kinds.size, 128), F32),
        in_specs=[pl.BlockSpec(memory_space=pltpu.SMEM), VMEM],
        out_specs=VMEM,
        compiler_params=PARAMS,
        name="wavenum",
    )(table, kinds)


def edge_rows(block, cells_y):
    cells = block.shape[0]
    row = lambda at, count: block[pl.ds(at, count)].astype(F32)
    return jnp.concatenate(
        [row(0, cells_y), row(cells - cells_y, cells_y)]
        + [row(x, 1) for x in range(0, cells, cells_y)]
        + [row(x + cells_y - 1, 1) for x in range(0, cells, cells_y)],
        axis=0,
    )


def volume_kernel(cells_y, weights, left, lower, volume, edges, edge_weights):
    volume[...] = product(weights, [left], lower)
    edges[...] = edge_rows(volume, cells_y).astype(BF16)
    edge_weights[...] = edge_rows(weights, cells_y).astype(BF16)


def volume_of(weights, left, lower, cells_y):
    width = left.shape[1]
    cells, depth = weights.shape
    lines = 2 * (cells_y + cells // cells_y)
    return pl.pallas_call(
        functools.partial(volume_kernel, cells_y),
        out_shape=(
            jax.ShapeDtypeStruct((cells, width), F32),
            jax.ShapeDtypeStruct((lines, width), BF16),
            jax.ShapeDtypeStruct((lines, depth), BF16),
        ),
        in_specs=[VMEM] * 3,
        out_specs=(VMEM,) * 3,
        cost_estimate=cost(2 * weights.size * width, 2 * weights.size + 4 * weights.shape[1] * width),
        compiler_params=PARAMS,
        name="volume",
    )(weights, left, lower)


def edges_kernel(weights, left, lower, done, x_pair, x_cross, y_pair, y_cross):
    old, width = done.shape[1], left.shape[1]
    fresh = product(weights, [left], lower).astype(BF16)
    even_x = lax.rem(lax.axis_index("gx"), 2) == 0
    even_y = lax.rem(lax.axis_index("gy"), 2) == 0
    deep, high = x_pair.shape[0], y_pair.shape[0]
    for where, block in ((pl.ds(0, old), done[...]), (pl.ds(old, width), fresh)):
        first, last = block[:deep], block[deep : 2 * deep]
        x_pair[:, where] = jnp.where(even_x, last, first)
        x_cross[:, where] = jnp.where(even_x, first, last)
        first, last = block[2 * deep : 2 * deep + high], block[2 * deep + high :]
        y_pair[:, where] = jnp.where(even_y, last, first)
        y_cross[:, where] = jnp.where(even_y, first, last)


def edges_of(weights, left, lower, done, cells_y):
    width = lower.shape[1]
    total = width + done.shape[1]
    line = lambda n: jax.ShapeDtypeStruct((n, total), BF16)
    cells_x = weights.shape[0] // 2 - cells_y
    return pl.pallas_call(
        edges_kernel,
        out_shape=(line(cells_y), line(cells_y), line(cells_x), line(cells_x)),
        in_specs=[VMEM] * 4,
        out_specs=(VMEM,) * 4,
        cost_estimate=cost(2 * weights.size * width, 2 * weights.size + 4 * weights.shape[1] * width),
        compiler_params=PARAMS,
        name="edges",
    )(weights, left, lower, done)


def last_kernel(z_top, z_low, left, lower, right_hbm, upper_hbm, right, upper, sem):
    width = left.shape[1]
    half = left.shape[0] // 2
    copies = []
    for z, out, out_hbm in ((z_top, right, right_hbm), (z_low, upper, upper_hbm)):
        for r in range(2):
            here = pl.ds(r * half, half)
            out[here] = product(z.at[here], [left], lower).astype(BF16)
            copies.append(
                pltpu.make_async_copy(out.at[here], out_hbm.at[here, pl.ds(0, width)], sem.at[len(copies)])
            )
            copies[-1].start()
    for copy in copies:
        copy.wait()


def last(z_top, z_low, left, lower, total):
    trace, width = left.shape
    out = jax.ShapeDtypeStruct((trace, total), BF16)
    return pl.pallas_call(
        last_kernel,
        out_shape=(out, out),
        in_specs=[VMEM] * 4,
        out_specs=(HBM, HBM),
        scratch_shapes=[
            pltpu.VMEM((trace, width), BF16),
            pltpu.VMEM((trace, width), BF16),
            pltpu.SemaphoreType.DMA((4,)),
        ],
        cost_estimate=cost(8 * trace * trace * width, 8 * trace * trace + 8 * trace * width),
        compiler_params=PARAMS,
        name="last",
    )(z_top, z_low, left, lower)


def plain_kernel(z_top, z_low, weights, left, lower, wavenum, first, *refs):
    right_hbm, inner, upper, right, second, sem = refs[-6:]
    left = [left]
    half, width = right.shape[0] // 2, right.shape[1]
    base = right_hbm.shape[1] - width
    copies = []
    for r in range(2):
        here = pl.ds(r * half, half)
        right[here] = product(z_top.at[here], left, lower).astype(BF16)
        copies.append(pltpu.make_async_copy(right.at[here], right_hbm.at[here, pl.ds(base, width)], sem.at[r]))
        copies[-1].start()
    for r in range(2):
        here = pl.ds(r * half, half)
        upper[here] = product(z_low.at[here], left, lower).astype(BF16)
    second[...] = product(weights, left, lower)
    cells_x, cells_y = inner.shape[:2]
    start = 0
    for volume in (first, second):
        where = pl.ds(start, volume.shape[1])
        start += volume.shape[1]
        place = lax.broadcasted_iota(jnp.int32, (cells_y, volume.shape[1]), 0)
        for x in range(cells_x):
            row = lambda k: volume[pl.ds(k * cells_y, cells_y)]
            here = row(x)
            around_it = jnp.where(place == 0, 0.0, pltpu.roll(here, 1, 0)) + jnp.where(
                place == cells_y - 1, 0.0, pltpu.roll(here, cells_y - 1, 0)
            )
            if x:
                around_it = around_it + row(x - 1)
            if x + 1 < cells_x:
                around_it = around_it + row(x + 1)
            scale = wavenum[pl.ds(x * cells_y, cells_y)][:, :1]
            inner[x, :, where] = around_it - 4.0 * here + scale * here
    for copy in copies:
        copy.wait()


def plain(z_top, z_low, weights, left, lower, wavenum, volume, before, cells_y):
    trace, width = lower.shape
    cells = volume.shape[0]
    total = before.shape[1]
    given = 7
    return pl.pallas_call(
        plain_kernel,
        out_shape=(
            jax.ShapeDtypeStruct(before.shape, before.dtype),
            jax.ShapeDtypeStruct((cells // cells_y, cells_y, total), F32),
            jax.ShapeDtypeStruct((trace, width), BF16),
        ),
        in_specs=[VMEM] * given + [HBM],
        out_specs=(HBM, VMEM, VMEM),
        scratch_shapes=[
            pltpu.VMEM((trace, width), BF16),
            pltpu.VMEM((cells, width), F32),
            pltpu.SemaphoreType.DMA((2,)),
        ],
        input_output_aliases={given: 0},
        cost_estimate=cost(8 * trace * trace * width, 8 * trace * trace + 8 * trace * width),
        compiler_params=PACKED,
        name="plain",
    )(z_top, z_low, weights, left, lower, wavenum, volume, before)


def beside(axis, pair, cross):
    place = lax.axis_index(axis)
    even = lax.rem(place, 2) == 0
    pair, cross = pair[...].astype(F32), cross[...].astype(F32)
    before = jnp.where(place == 0, 0.0, jnp.where(even, cross, pair))
    after = jnp.where(is_last(axis), 0.0, jnp.where(even, pair, cross))
    return before, after


def finish_kernel(inner, upper, x_pair, x_cross, y_pair, y_cross, _, upper_hbm, residual_hbm, out, sem):
    cells_x, cells_y, total = inner.shape
    groups = sem.shape[0] - 1
    deep = cells_x // groups
    before_x, after_x = beside("gx", x_pair, x_cross)
    before_y, after_y = beside("gy", y_pair, y_cross)
    place = lax.broadcasted_iota(jnp.int32, (cells_y, total), 0)
    width = upper.shape[1]
    base = upper_hbm.shape[1] - width
    copies = [pltpu.make_async_copy(upper, upper_hbm.at[:, pl.ds(base, width)], sem.at[groups])]
    copies[0].start()
    for group in range(groups):
        for x in range(group * deep, (group + 1) * deep):
            value = inner[x]
            value = value + jnp.where(
                place == 0, before_y[x : x + 1], jnp.where(place == cells_y - 1, after_y[x : x + 1], 0.0)
            )
            if x == 0:
                value = value + before_x
            if x == cells_x - 1:
                value = value + after_x
            out[x] = value
        here = pl.ds(group * deep, deep)
        copies.append(pltpu.make_async_copy(out.at[here], residual_hbm.at[here], sem.at[group]))
        copies[-1].start()
    for copy in copies:
        copy.wait()


def finish(inner, upper, halos, before):
    groups = 2 if inner.shape[0] % 2 == 0 else 1
    given = 2 + len(halos)
    return pl.pallas_call(
        finish_kernel,
        out_shape=(jax.ShapeDtypeStruct(before.shape, before.dtype), jax.ShapeDtypeStruct(inner.shape, F32)),
        in_specs=[VMEM] * given + [HBM],
        out_specs=(HBM, HBM),
        scratch_shapes=[pltpu.VMEM(inner.shape, F32), pltpu.SemaphoreType.DMA((groups + 1,))],
        input_output_aliases={given: 0},
        cost_estimate=cost(4 * inner.size, 8 * inner.size),
        compiler_params=PARAMS,
        name="finish",
    )(inner, upper, *halos, before)


def per_device(impedance, rebuild_map, left_trace, lower_trace, cell_kind, kind_wavenum):
    z = pltpu.with_memory_space_constraint(impedance[0, 0], pltpu.HBM)
    weights = rebuild_map[0, 0]
    left_all = pltpu.with_memory_space_constraint(left_trace[0, 0], pltpu.HBM)
    lower_all = pltpu.with_memory_space_constraint(lower_trace[0, 0], pltpu.HBM)
    sources = left_all.shape[1]
    width = sources // CHUNKS
    _, cells_y = cell_kind.shape
    left_in, lower_in = [None] * CHUNKS, [None] * CHUNKS
    for step in range(STEPS - 1):
        for c in range(CHUNKS):
            if step == 0 and c == 0:
                right, z_top, left, lower = first_right(z, left_all, lower_all, 0, width)
            elif step == 0:
                right, left, lower = part_loading("gx", z_top, left_all, lower_all, c * width, width)
            else:
                left, lower = left_in[c], lower_in[c]
                right = part("gx", z_top, left, lower)
            final = step == STEPS - 2 and c == CHUNKS - 1
            left_in[c] = onward(right, "gx") if final else around(right, "gx")
            if step == 0 and c == 0:
                upper, z_low = first_upper(z, left, lower)
            else:
                upper = part("gy", z_low, left, lower)
            lower_in[c] = around(upper, "gy")

    wavenum = wavenum_of(kind_wavenum, cell_kind)
    volume, edges, edge_weights = volume_of(weights, left_in[0], lower_in[0], cells_y)
    outs = last(z_top, z_low, left_in[0], lower_in[0], sources)
    volume, wavenum, left, lower, *outs = lax.optimization_barrier(
        (volume, wavenum, left_in[1], lower_in[1], *outs)
    )
    x_pair, x_cross, y_pair, y_cross = edges_of(edge_weights, left, lower, edges, cells_y)
    x_pair = swapped(x_pair, "gx", 0)
    x_cross = swapped(x_cross, "gx", 1)
    y_cross = swapped(y_cross, "gy", 1)
    y_pair = swapped(y_pair, "gy", 0)
    halos = (x_pair, x_cross, y_pair, y_cross)
    right_out, inner, upper = plain(z_top, z_low, weights, left, lower, wavenum, volume, outs[0], cells_y)
    upper_out, residual = finish(inner, upper, halos, outs[1])
    return (right_out[None, None], upper_out[None, None], residual)


def solution(mesh):
    return jax.shard_map(
        per_device,
        mesh=mesh,
        in_specs=(
            P("gx", "gy", None, None),
            P("gx", "gy", None, None),
            P("gx", "gy", None, None),
            P("gx", "gy", None, None),
            P("gx", "gy"),
            P(),
        ),
        out_specs=(P("gx", "gy", None, None), P("gx", "gy", None, None), P("gx", "gy", None)),
        check_vma=False,
    )
```

```python
import functools

import jax
import jax.numpy as jnp
from jax import lax
from jax.experimental import pallas as pl
from jax.experimental.pallas import tpu as pltpu
from jax.sharding import PartitionSpec as P


STEPS = 4
CHUNKS = 2
F32 = jnp.float32
BF16 = jnp.bfloat16
VMEM = pl.BlockSpec(memory_space=pltpu.VMEM)
HBM = pl.BlockSpec(memory_space=pltpu.HBM)


def around(block, axis):
    count = lax.axis_size(axis)
    return lax.ppermute(block, axis, [(i, (i + 1) % count) for i in range(count)])


def onward(block, axis):
    count = lax.axis_size(axis)
    return lax.ppermute(block, axis, [(i, i + 1) for i in range(count - 1)])


def swapped(block, axis, first):
    names = ("gx", "gy")
    along = names.index(axis)
    sizes = tuple(lax.axis_size(name) for name in names)
    pairs = []
    for place in range(sizes[0] * sizes[1]):
        where = [place // sizes[1], place % sizes[1]]
        mate = first + ((where[along] - first) ^ 1)
        if 0 <= mate < sizes[along]:
            where[along] = mate
        elif axis == "gy":
            where[along] = sizes[along] - 1 - where[along]
        else:
            where[1 - along] ^= 1
        pairs.append((place, where[0] * sizes[1] + where[1]))
    return lax.ppermute(block, names, pairs)


def is_last(axis):
    return lax.axis_index(axis) == lax.axis_size(axis) - 1


PARAMS = pltpu.CompilerParams(vmem_limit_bytes=6 * 2**20)
PACKED = pltpu.CompilerParams(vmem_limit_bytes=6 * 2**20)


def cost(flops, moved):
    return pl.CostEstimate(flops=int(flops), bytes_accessed=int(moved), transcendentals=0)


def product(weights, left, lower):
    total, start = None, 0
    for piece in (*left, lower):
        rows = piece.shape[0]
        share = jnp.dot(weights[:, start : start + rows], piece[...], preferred_element_type=F32)
        total = share if total is None else total + share
        start += rows
    return total


def first_right_kernel(base, width, z_hbm, left_hbm, lower_hbm, out, z_top, left, lower, sem):
    rows = z_top.shape[0]
    block = rows // 2
    loads = [
        pltpu.make_async_copy(left_hbm.at[:, pl.ds(base, width)], left, sem.at[0]),
        pltpu.make_async_copy(lower_hbm.at[:, pl.ds(base, width)], lower, sem.at[1]),
    ]
    parts = [
        pltpu.make_async_copy(z_hbm.at[pl.ds(r * block, block)], z_top.at[pl.ds(r * block, block)], sem.at[2 + r])
        for r in range(2)
    ]
    for copy in loads + parts:
        copy.start()
    for copy in loads:
        copy.wait()
    at_end = is_last("gx")
    for r in range(2):
        parts[r].wait()
        here = pl.ds(r * block, block)
        out[here] = jnp.where(at_end, 0.0, product(z_top.at[here], [left], lower)).astype(BF16)


def first_right(z, left, lower, base, width):
    trace = left.shape[0]
    vmem = lambda *shape: jax.ShapeDtypeStruct(shape, BF16)
    return pl.pallas_call(
        functools.partial(first_right_kernel, base, width),
        out_shape=(vmem(trace, width), vmem(trace, 2 * trace), vmem(trace, width), vmem(trace, width)),
        in_specs=[HBM, HBM, HBM],
        out_specs=(VMEM,) * 4,
        scratch_shapes=[pltpu.SemaphoreType.DMA((4,))],
        cost_estimate=cost(4 * trace * trace * width, 4 * trace * trace + 6 * trace * width),
        compiler_params=PACKED,
        name="first_right",
    )(z, left, lower)


def first_upper_kernel(z_hbm, left, lower, out, z_low, sem):
    rows = z_low.shape[0]
    block = rows // 2
    parts = [
        pltpu.make_async_copy(z_hbm.at[pl.ds(rows + r * block, block)], z_low.at[pl.ds(r * block, block)], sem.at[r])
        for r in range(2)
    ]
    for copy in parts:
        copy.start()
    at_end = is_last("gy")
    for r in range(2):
        parts[r].wait()
        here = pl.ds(r * block, block)
        out[here] = jnp.where(at_end, 0.0, product(z_low.at[here], [left], lower)).astype(BF16)


def first_upper(z, left, lower):
    trace, width = left.shape
    vmem = lambda *shape: jax.ShapeDtypeStruct(shape, BF16)
    return pl.pallas_call(
        first_upper_kernel,
        out_shape=(vmem(trace, width), vmem(trace, 2 * trace)),
        in_specs=[HBM, VMEM, VMEM],
        out_specs=(VMEM,) * 2,
        scratch_shapes=[pltpu.SemaphoreType.DMA((2,))],
        cost_estimate=cost(4 * trace * trace * width, 4 * trace * trace + 6 * trace * width),
        compiler_params=PARAMS,
        name="first_upper",
    )(z, left, lower)


def part_kernel(axis, z, left, lower, out):
    half = left.shape[0] // 2
    at_end = is_last(axis)
    for r in range(2):
        here = pl.ds(r * half, half)
        out[here] = jnp.where(at_end, 0.0, product(z.at[here], [left], lower)).astype(BF16)


def part(axis, z, left, lower):
    trace, width = left.shape
    return pl.pallas_call(
        functools.partial(part_kernel, axis),
        out_shape=jax.ShapeDtypeStruct((trace, width), BF16),
        in_specs=[VMEM] * 3,
        out_specs=VMEM,
        cost_estimate=cost(4 * trace * trace * width, 4 * trace * trace + 6 * trace * width),
        compiler_params=PACKED,
        name="part",
    )(z, left, lower)


def part_loading_kernel(axis, base, z, left_hbm, lower_hbm, out, left, lower, sem):
    width = left.shape[1]
    loads = [
        pltpu.make_async_copy(left_hbm.at[:, pl.ds(base, width)], left, sem.at[0]),
        pltpu.make_async_copy(lower_hbm.at[:, pl.ds(base, width)], lower, sem.at[1]),
    ]
    for copy in loads:
        copy.start()
    for copy in loads:
        copy.wait()
    part_kernel(axis, z, left, lower, out)


def part_loading(axis, z, left, lower, base, width):
    trace = left.shape[0]
    block = jax.ShapeDtypeStruct((trace, width), BF16)
    return pl.pallas_call(
        functools.partial(part_loading_kernel, axis, base),
        out_shape=(block,) * 3,
        in_specs=[VMEM, HBM, HBM],
        out_specs=(VMEM,) * 3,
        scratch_shapes=[pltpu.SemaphoreType.DMA((2,))],
        cost_estimate=cost(4 * trace * trace * width, 4 * trace * trace + 6 * trace * width),
        compiler_params=PACKED,
        name="part_loading",
    )(z, left, lower)


def wavenum_kernel(table, kinds, out):
    cells_x, cells_y = kinds.shape
    kind = kinds[...]
    value = jnp.zeros(kind.shape, F32)
    for k in range(table.shape[0]):
        value = jnp.where(kind == k, table[k], value)
    shape = (cells_y, cells_y)
    diagonal = lax.broadcasted_iota(jnp.int32, shape, 0) == lax.broadcasted_iota(jnp.int32, shape, 1)
    for x in range(cells_x):
        column = jnp.sum(jnp.where(diagonal, value[x : x + 1], 0.0), axis=1, keepdims=True)
        out[pl.ds(x * cells_y, cells_y)] = jnp.broadcast_to(column, (cells_y, out.shape[1]))


def wavenum_of(table, kinds):
    return pl.pallas_call(
        wavenum_kernel,
        out_shape=jax.ShapeDtypeStruct((kinds.size, 128), F32),
        in_specs=[pl.BlockSpec(memory_space=pltpu.SMEM), VMEM],
        out_specs=VMEM,
        compiler_params=PARAMS,
        name="wavenum",
    )(table, kinds)


def edge_rows(block, cells_y):
    cells = block.shape[0]
    row = lambda at, count: block[pl.ds(at, count)].astype(F32)
    return jnp.concatenate(
        [row(0, cells_y), row(cells - cells_y, cells_y)]
        + [row(x, 1) for x in range(0, cells, cells_y)]
        + [row(x + cells_y - 1, 1) for x in range(0, cells, cells_y)],
        axis=0,
    )


def volume_kernel(cells_y, weights, left, lower, volume, edges, edge_weights):
    volume[...] = product(weights, [left], lower)
    edges[...] = edge_rows(volume, cells_y).astype(BF16)
    edge_weights[...] = edge_rows(weights, cells_y).astype(BF16)


def volume_of(weights, left, lower, cells_y):
    width = left.shape[1]
    cells, depth = weights.shape
    lines = 2 * (cells_y + cells // cells_y)
    return pl.pallas_call(
        functools.partial(volume_kernel, cells_y),
        out_shape=(
            jax.ShapeDtypeStruct((cells, width), F32),
            jax.ShapeDtypeStruct((lines, width), BF16),
            jax.ShapeDtypeStruct((lines, depth), BF16),
        ),
        in_specs=[VMEM] * 3,
        out_specs=(VMEM,) * 3,
        cost_estimate=cost(2 * weights.size * width, 2 * weights.size + 4 * weights.shape[1] * width),
        compiler_params=PARAMS,
        name="volume",
    )(weights, left, lower)


def edges_kernel(weights, left, lower, done, x_pair, x_cross, y_pair, y_cross):
    old, width = done.shape[1], left.shape[1]
    fresh = product(weights, [left], lower).astype(BF16)
    even_x = lax.rem(lax.axis_index("gx"), 2) == 0
    even_y = lax.rem(lax.axis_index("gy"), 2) == 0
    deep, high = x_pair.shape[0], y_pair.shape[0]
    for where, block in ((pl.ds(0, old), done[...]), (pl.ds(old, width), fresh)):
        first, last = block[:deep], block[deep : 2 * deep]
        x_pair[:, where] = jnp.where(even_x, last, first)
        x_cross[:, where] = jnp.where(even_x, first, last)
        first, last = block[2 * deep : 2 * deep + high], block[2 * deep + high :]
        y_pair[:, where] = jnp.where(even_y, last, first)
        y_cross[:, where] = jnp.where(even_y, first, last)


def edges_of(weights, left, lower, done, cells_y):
    width = lower.shape[1]
    total = width + done.shape[1]
    line = lambda n: jax.ShapeDtypeStruct((n, total), BF16)
    cells_x = weights.shape[0] // 2 - cells_y
    return pl.pallas_call(
        edges_kernel,
        out_shape=(line(cells_y), line(cells_y), line(cells_x), line(cells_x)),
        in_specs=[VMEM] * 4,
        out_specs=(VMEM,) * 4,
        cost_estimate=cost(2 * weights.size * width, 2 * weights.size + 4 * weights.shape[1] * width),
        compiler_params=PACKED,
        name="edges",
    )(weights, left, lower, done)


def last_kernel(z_top, z_low, left, lower, right_hbm, upper_hbm, right, upper, sem):
    width = left.shape[1]
    half = left.shape[0] // 2
    copies = []
    for z, out, out_hbm in ((z_top, right, right_hbm), (z_low, upper, upper_hbm)):
        for r in range(2):
            here = pl.ds(r * half, half)
            out[here] = product(z.at[here], [left], lower).astype(BF16)
            copies.append(
                pltpu.make_async_copy(out.at[here], out_hbm.at[here, pl.ds(0, width)], sem.at[len(copies)])
            )
            copies[-1].start()
    for copy in copies:
        copy.wait()


def last(z_top, z_low, left, lower, total):
    trace, width = left.shape
    out = jax.ShapeDtypeStruct((trace, total), BF16)
    return pl.pallas_call(
        last_kernel,
        out_shape=(out, out),
        in_specs=[VMEM] * 4,
        out_specs=(HBM, HBM),
        scratch_shapes=[
            pltpu.VMEM((trace, width), BF16),
            pltpu.VMEM((trace, width), BF16),
            pltpu.SemaphoreType.DMA((4,)),
        ],
        cost_estimate=cost(8 * trace * trace * width, 8 * trace * trace + 8 * trace * width),
        compiler_params=PACKED,
        name="last",
    )(z_top, z_low, left, lower)


def plain_kernel(z_top, z_low, weights, left, lower, wavenum, first, *refs):
    right_hbm, inner, upper, right, second, sem = refs[-6:]
    left = [left]
    half, width = right.shape[0] // 2, right.shape[1]
    base = right_hbm.shape[1] - width
    copies = []
    for r in range(2):
        here = pl.ds(r * half, half)
        right[here] = product(z_top.at[here], left, lower).astype(BF16)
        copies.append(pltpu.make_async_copy(right.at[here], right_hbm.at[here, pl.ds(base, width)], sem.at[r]))
        copies[-1].start()
    for r in range(2):
        here = pl.ds(r * half, half)
        upper[here] = product(z_low.at[here], left, lower).astype(BF16)
    second[...] = product(weights, left, lower)
    cells_x, cells_y = inner.shape[:2]
    start = 0
    for volume in (first, second):
        where = pl.ds(start, volume.shape[1])
        start += volume.shape[1]
        place = lax.broadcasted_iota(jnp.int32, (cells_y, volume.shape[1]), 0)
        for x in range(cells_x):
            row = lambda k: volume[pl.ds(k * cells_y, cells_y)]
            here = row(x)
            around_it = jnp.where(place == 0, 0.0, pltpu.roll(here, 1, 0)) + jnp.where(
                place == cells_y - 1, 0.0, pltpu.roll(here, cells_y - 1, 0)
            )
            if x:
                around_it = around_it + row(x - 1)
            if x + 1 < cells_x:
                around_it = around_it + row(x + 1)
            scale = wavenum[pl.ds(x * cells_y, cells_y)][:, :1]
            inner[x, :, where] = around_it - 4.0 * here + scale * here
    for copy in copies:
        copy.wait()


def plain(z_top, z_low, weights, left, lower, wavenum, volume, before, cells_y):
    trace, width = lower.shape
    cells = volume.shape[0]
    total = before.shape[1]
    given = 7
    return pl.pallas_call(
        plain_kernel,
        out_shape=(
            jax.ShapeDtypeStruct(before.shape, before.dtype),
            jax.ShapeDtypeStruct((cells // cells_y, cells_y, total), F32),
            jax.ShapeDtypeStruct((trace, width), BF16),
        ),
        in_specs=[VMEM] * given + [HBM],
        out_specs=(HBM, VMEM, VMEM),
        scratch_shapes=[
            pltpu.VMEM((trace, width), BF16),
            pltpu.VMEM((cells, width), F32),
            pltpu.SemaphoreType.DMA((2,)),
        ],
        input_output_aliases={given: 0},
        cost_estimate=cost(8 * trace * trace * width, 8 * trace * trace + 8 * trace * width),
        compiler_params=PACKED,
        name="plain",
    )(z_top, z_low, weights, left, lower, wavenum, volume, before)


def beside(axis, pair, cross):
    place = lax.axis_index(axis)
    even = lax.rem(place, 2) == 0
    pair, cross = pair[...].astype(F32), cross[...].astype(F32)
    before = jnp.where(place == 0, 0.0, jnp.where(even, cross, pair))
    after = jnp.where(is_last(axis), 0.0, jnp.where(even, pair, cross))
    return before, after


def finish_kernel(inner, upper, x_pair, x_cross, y_pair, y_cross, _, upper_hbm, residual_hbm, out, sem):
    cells_x, cells_y, total = inner.shape
    groups = sem.shape[0] - 1
    deep = cells_x // groups
    before_x, after_x = beside("gx", x_pair, x_cross)
    before_y, after_y = beside("gy", y_pair, y_cross)
    place = lax.broadcasted_iota(jnp.int32, (cells_y, total), 0)
    width = upper.shape[1]
    base = upper_hbm.shape[1] - width
    copies = [pltpu.make_async_copy(upper, upper_hbm.at[:, pl.ds(base, width)], sem.at[groups])]
    copies[0].start()
    for group in range(groups):
        for x in range(group * deep, (group + 1) * deep):
            value = inner[x]
            value = value + jnp.where(
                place == 0, before_y[x : x + 1], jnp.where(place == cells_y - 1, after_y[x : x + 1], 0.0)
            )
            if x == 0:
                value = value + before_x
            if x == cells_x - 1:
                value = value + after_x
            out[x] = value
        here = pl.ds(group * deep, deep)
        copies.append(pltpu.make_async_copy(out.at[here], residual_hbm.at[here], sem.at[group]))
        copies[-1].start()
    for copy in copies:
        copy.wait()


def finish(inner, upper, halos, before):
    groups = 2 if inner.shape[0] % 2 == 0 else 1
    given = 2 + len(halos)
    return pl.pallas_call(
        finish_kernel,
        out_shape=(jax.ShapeDtypeStruct(before.shape, before.dtype), jax.ShapeDtypeStruct(inner.shape, F32)),
        in_specs=[VMEM] * given + [HBM],
        out_specs=(HBM, HBM),
        scratch_shapes=[pltpu.VMEM(inner.shape, F32), pltpu.SemaphoreType.DMA((groups + 1,))],
        input_output_aliases={given: 0},
        cost_estimate=cost(4 * inner.size, 8 * inner.size),
        compiler_params=PARAMS,
        name="finish",
    )(inner, upper, *halos, before)


def per_device(impedance, rebuild_map, left_trace, lower_trace, cell_kind, kind_wavenum):
    z = pltpu.with_memory_space_constraint(impedance[0, 0], pltpu.HBM)
    weights = rebuild_map[0, 0]
    left_all = pltpu.with_memory_space_constraint(left_trace[0, 0], pltpu.HBM)
    lower_all = pltpu.with_memory_space_constraint(lower_trace[0, 0], pltpu.HBM)
    sources = left_all.shape[1]
    width = sources // CHUNKS
    _, cells_y = cell_kind.shape
    left_in, lower_in = [None] * CHUNKS, [None] * CHUNKS
    for step in range(STEPS - 1):
        for c in range(CHUNKS):
            if step == 0 and c == 0:
                right, z_top, left, lower = first_right(z, left_all, lower_all, 0, width)
            elif step == 0:
                right, left, lower = part_loading("gx", z_top, left_all, lower_all, c * width, width)
            else:
                left, lower = left_in[c], lower_in[c]
                right = part("gx", z_top, left, lower)
            final = step == STEPS - 2 and c == CHUNKS - 1
            left_in[c] = onward(right, "gx") if final else around(right, "gx")
            if step == 0 and c == 0:
                upper, z_low = first_upper(z, left, lower)
            else:
                upper = part("gy", z_low, left, lower)
            lower_in[c] = around(upper, "gy")

    wavenum = wavenum_of(kind_wavenum, cell_kind)
    volume, edges, edge_weights = volume_of(weights, left_in[0], lower_in[0], cells_y)
    outs = last(z_top, z_low, left_in[0], lower_in[0], sources)
    volume, wavenum, left, lower, *outs = lax.optimization_barrier(
        (volume, wavenum, left_in[1], lower_in[1], *outs)
    )
    x_pair, x_cross, y_pair, y_cross = edges_of(edge_weights, left, lower, edges, cells_y)
    x_pair = swapped(x_pair, "gx", 0)
    x_cross = swapped(x_cross, "gx", 1)
    y_cross = swapped(y_cross, "gy", 1)
    y_pair = swapped(y_pair, "gy", 0)
    halos = (x_pair, x_cross, y_pair, y_cross)
    right_out, inner, upper = plain(z_top, z_low, weights, left, lower, wavenum, volume, outs[0], cells_y)
    upper_out, residual = finish(inner, upper, halos, outs[1])
    return (right_out[None, None], upper_out[None, None], residual)


def solution(mesh):
    return jax.shard_map(
        per_device,
        mesh=mesh,
        in_specs=(
            P("gx", "gy", None, None),
            P("gx", "gy", None, None),
            P("gx", "gy", None, None),
            P("gx", "gy", None, None),
            P("gx", "gy"),
            P(),
        ),
        out_specs=(P("gx", "gy", None, None), P("gx", "gy", None, None), P("gx", "gy", None)),
        check_vma=False,
    )
```

```python
import functools

import jax
import jax.numpy as jnp
from jax import lax
from jax.experimental import pallas as pl
from jax.experimental.pallas import tpu as pltpu
from jax.sharding import PartitionSpec as P


STEPS = 4
CHUNKS = 2
F32 = jnp.float32
BF16 = jnp.bfloat16
VMEM = pl.BlockSpec(memory_space=pltpu.VMEM)
HBM = pl.BlockSpec(memory_space=pltpu.HBM)


def around(block, axis):
    count = lax.axis_size(axis)
    return lax.ppermute(block, axis, [(i, (i + 1) % count) for i in range(count)])


def onward(block, axis):
    count = lax.axis_size(axis)
    return lax.ppermute(block, axis, [(i, i + 1) for i in range(count - 1)])


def swapped(block, axis, first):
    names = ("gx", "gy")
    along = names.index(axis)
    sizes = tuple(lax.axis_size(name) for name in names)
    pairs = []
    for place in range(sizes[0] * sizes[1]):
        where = [place // sizes[1], place % sizes[1]]
        mate = first + ((where[along] - first) ^ 1)
        if 0 <= mate < sizes[along]:
            where[along] = mate
        elif axis == "gy":
            where[along] = sizes[along] - 1 - where[along]
        else:
            where[1 - along] ^= 1
        pairs.append((place, where[0] * sizes[1] + where[1]))
    return lax.ppermute(block, names, pairs)


def is_last(axis):
    return lax.axis_index(axis) == lax.axis_size(axis) - 1


PARAMS = pltpu.CompilerParams(vmem_limit_bytes=6 * 2**20)
PACKED = pltpu.CompilerParams(vmem_limit_bytes=6 * 2**20)


def cost(flops, moved):
    return pl.CostEstimate(flops=int(flops), bytes_accessed=int(moved), transcendentals=0)


def product(weights, left, lower):
    total, start = None, 0
    for piece in (*left, lower):
        rows = piece.shape[0]
        share = jnp.dot(weights[:, start : start + rows], piece[...], preferred_element_type=F32)
        total = share if total is None else total + share
        start += rows
    return total


def first_right_kernel(base, width, z_hbm, left_hbm, lower_hbm, out, z_top, left, lower, sem):
    rows = z_top.shape[0]
    block = rows // 2
    loads = [
        pltpu.make_async_copy(left_hbm.at[:, pl.ds(base, width)], left, sem.at[0]),
        pltpu.make_async_copy(lower_hbm.at[:, pl.ds(base, width)], lower, sem.at[1]),
    ]
    parts = [
        pltpu.make_async_copy(z_hbm.at[pl.ds(r * block, block)], z_top.at[pl.ds(r * block, block)], sem.at[2 + r])
        for r in range(2)
    ]
    for copy in loads + parts:
        copy.start()
    for copy in loads:
        copy.wait()
    at_end = is_last("gx")
    for r in range(2):
        parts[r].wait()
        here = pl.ds(r * block, block)
        out[here] = jnp.where(at_end, 0.0, product(z_top.at[here], [left], lower)).astype(BF16)


def first_right(z, left, lower, base, width):
    trace = left.shape[0]
    vmem = lambda *shape: jax.ShapeDtypeStruct(shape, BF16)
    return pl.pallas_call(
        functools.partial(first_right_kernel, base, width),
        out_shape=(vmem(trace, width), vmem(trace, 2 * trace), vmem(trace, width), vmem(trace, width)),
        in_specs=[HBM, HBM, HBM],
        out_specs=(VMEM,) * 4,
        scratch_shapes=[pltpu.SemaphoreType.DMA((4,))],
        cost_estimate=cost(4 * trace * trace * width, 4 * trace * trace + 6 * trace * width),
        compiler_params=PARAMS,
        name="first_right",
    )(z, left, lower)


def first_upper_kernel(z_hbm, left, lower, out, z_low, sem):
    rows = z_low.shape[0]
    block = rows // 2
    parts = [
        pltpu.make_async_copy(z_hbm.at[pl.ds(rows + r * block, block)], z_low.at[pl.ds(r * block, block)], sem.at[r])
        for r in range(2)
    ]
    for copy in parts:
        copy.start()
    at_end = is_last("gy")
    for r in range(2):
        parts[r].wait()
        here = pl.ds(r * block, block)
        out[here] = jnp.where(at_end, 0.0, product(z_low.at[here], [left], lower)).astype(BF16)


def first_upper(z, left, lower):
    trace, width = left.shape
    vmem = lambda *shape: jax.ShapeDtypeStruct(shape, BF16)
    return pl.pallas_call(
        first_upper_kernel,
        out_shape=(vmem(trace, width), vmem(trace, 2 * trace)),
        in_specs=[HBM, VMEM, VMEM],
        out_specs=(VMEM,) * 2,
        scratch_shapes=[pltpu.SemaphoreType.DMA((2,))],
        cost_estimate=cost(4 * trace * trace * width, 4 * trace * trace + 6 * trace * width),
        compiler_params=PARAMS,
        name="first_upper",
    )(z, left, lower)


def part_kernel(axis, z, left, lower, out):
    half = left.shape[0] // 2
    at_end = is_last(axis)
    for r in range(2):
        here = pl.ds(r * half, half)
        out[here] = jnp.where(at_end, 0.0, product(z.at[here], [left], lower)).astype(BF16)


def part(axis, z, left, lower):
    trace, width = left.shape
    return pl.pallas_call(
        functools.partial(part_kernel, axis),
        out_shape=jax.ShapeDtypeStruct((trace, width), BF16),
        in_specs=[VMEM] * 3,
        out_specs=VMEM,
        cost_estimate=cost(4 * trace * trace * width, 4 * trace * trace + 6 * trace * width),
        compiler_params=PARAMS,
        name="part",
    )(z, left, lower)


def part_loading_kernel(axis, base, z, left_hbm, lower_hbm, out, left, lower, sem):
    width = left.shape[1]
    loads = [
        pltpu.make_async_copy(left_hbm.at[:, pl.ds(base, width)], left, sem.at[0]),
        pltpu.make_async_copy(lower_hbm.at[:, pl.ds(base, width)], lower, sem.at[1]),
    ]
    for copy in loads:
        copy.start()
    for copy in loads:
        copy.wait()
    part_kernel(axis, z, left, lower, out)


def part_loading(axis, z, left, lower, base, width):
    trace = left.shape[0]
    block = jax.ShapeDtypeStruct((trace, width), BF16)
    return pl.pallas_call(
        functools.partial(part_loading_kernel, axis, base),
        out_shape=(block,) * 3,
        in_specs=[VMEM, HBM, HBM],
        out_specs=(VMEM,) * 3,
        scratch_shapes=[pltpu.SemaphoreType.DMA((2,))],
        cost_estimate=cost(4 * trace * trace * width, 4 * trace * trace + 6 * trace * width),
        compiler_params=PARAMS,
        name="part_loading",
    )(z, left, lower)


def wavenum_kernel(table, kinds, out):
    cells_x, cells_y = kinds.shape
    kind = kinds[...]
    value = jnp.zeros(kind.shape, F32)
    for k in range(table.shape[0]):
        value = jnp.where(kind == k, table[k], value)
    shape = (cells_y, cells_y)
    diagonal = lax.broadcasted_iota(jnp.int32, shape, 0) == lax.broadcasted_iota(jnp.int32, shape, 1)
    for x in range(cells_x):
        column = jnp.sum(jnp.where(diagonal, value[x : x + 1], 0.0), axis=1, keepdims=True)
        out[pl.ds(x * cells_y, cells_y)] = jnp.broadcast_to(column, (cells_y, out.shape[1]))


def wavenum_of(table, kinds):
    return pl.pallas_call(
        wavenum_kernel,
        out_shape=jax.ShapeDtypeStruct((kinds.size, 128), F32),
        in_specs=[pl.BlockSpec(memory_space=pltpu.SMEM), VMEM],
        out_specs=VMEM,
        compiler_params=PARAMS,
        name="wavenum",
    )(table, kinds)


def edge_rows(block, cells_y):
    cells = block.shape[0]
    row = lambda at, count: block[pl.ds(at, count)].astype(F32)
    return jnp.concatenate(
        [row(0, cells_y), row(cells - cells_y, cells_y)]
        + [row(x, 1) for x in range(0, cells, cells_y)]
        + [row(x + cells_y - 1, 1) for x in range(0, cells, cells_y)],
        axis=0,
    )


def volume_kernel(cells_y, weights, left, lower, volume, edges, edge_weights):
    volume[...] = product(weights, [left], lower)
    edges[...] = edge_rows(volume, cells_y).astype(BF16)
    edge_weights[...] = edge_rows(weights, cells_y).astype(BF16)


def volume_of(weights, left, lower, cells_y):
    width = left.shape[1]
    cells, depth = weights.shape
    lines = 2 * (cells_y + cells // cells_y)
    return pl.pallas_call(
        functools.partial(volume_kernel, cells_y),
        out_shape=(
            jax.ShapeDtypeStruct((cells, width), F32),
            jax.ShapeDtypeStruct((lines, width), BF16),
            jax.ShapeDtypeStruct((lines, depth), BF16),
        ),
        in_specs=[VMEM] * 3,
        out_specs=(VMEM,) * 3,
        cost_estimate=cost(2 * weights.size * width, 2 * weights.size + 4 * weights.shape[1] * width),
        compiler_params=PARAMS,
        name="volume",
    )(weights, left, lower)


def edges_kernel(weights, left, lower, done, x_pair, x_cross, y_pair, y_cross):
    old, width = done.shape[1], left.shape[1]
    fresh = product(weights, [left], lower).astype(BF16)
    even_x = lax.rem(lax.axis_index("gx"), 2) == 0
    even_y = lax.rem(lax.axis_index("gy"), 2) == 0
    deep, high = x_pair.shape[0], y_pair.shape[0]
    for where, block in ((pl.ds(0, old), done[...]), (pl.ds(old, width), fresh)):
        first, last = block[:deep], block[deep : 2 * deep]
        x_pair[:, where] = jnp.where(even_x, last, first)
        x_cross[:, where] = jnp.where(even_x, first, last)
        first, last = block[2 * deep : 2 * deep + high], block[2 * deep + high :]
        y_pair[:, where] = jnp.where(even_y, last, first)
        y_cross[:, where] = jnp.where(even_y, first, last)


def edges_of(weights, left, lower, done, cells_y):
    width = lower.shape[1]
    total = width + done.shape[1]
    line = lambda n: jax.ShapeDtypeStruct((n, total), BF16)
    cells_x = weights.shape[0] // 2 - cells_y
    return pl.pallas_call(
        edges_kernel,
        out_shape=(line(cells_y), line(cells_y), line(cells_x), line(cells_x)),
        in_specs=[VMEM] * 4,
        out_specs=(VMEM,) * 4,
        cost_estimate=cost(2 * weights.size * width, 2 * weights.size + 4 * weights.shape[1] * width),
        compiler_params=PARAMS,
        name="edges",
    )(weights, left, lower, done)


def last_kernel(z_top, z_low, left, lower, right_hbm, upper_hbm, right, upper, sem):
    width = left.shape[1]
    half = left.shape[0] // 2
    copies = []
    for z, out, out_hbm in ((z_top, right, right_hbm), (z_low, upper, upper_hbm)):
        for r in range(2):
            here = pl.ds(r * half, half)
            out[here] = product(z.at[here], [left], lower).astype(BF16)
            copies.append(
                pltpu.make_async_copy(out.at[here], out_hbm.at[here, pl.ds(0, width)], sem.at[len(copies)])
            )
            copies[-1].start()
    for copy in copies:
        copy.wait()


def last(z_top, z_low, left, lower, total):
    trace, width = left.shape
    out = jax.ShapeDtypeStruct((trace, total), BF16)
    return pl.pallas_call(
        last_kernel,
        out_shape=(out, out),
        in_specs=[VMEM] * 4,
        out_specs=(HBM, HBM),
        scratch_shapes=[
            pltpu.VMEM((trace, width), BF16),
            pltpu.VMEM((trace, width), BF16),
            pltpu.SemaphoreType.DMA((4,)),
        ],
        cost_estimate=cost(8 * trace * trace * width, 8 * trace * trace + 8 * trace * width),
        compiler_params=PARAMS,
        name="last",
    )(z_top, z_low, left, lower)


def plain_kernel(z_top, z_low, weights, left, lower, wavenum, first, *refs):
    right_hbm, inner, upper, right, second, sem = refs[-6:]
    left = [left]
    half, width = right.shape[0] // 2, right.shape[1]
    base = right_hbm.shape[1] - width
    copies = []
    for r in range(2):
        here = pl.ds(r * half, half)
        right[here] = product(z_top.at[here], left, lower).astype(BF16)
        copies.append(pltpu.make_async_copy(right.at[here], right_hbm.at[here, pl.ds(base, width)], sem.at[r]))
        copies[-1].start()
    for r in range(2):
        here = pl.ds(r * half, half)
        upper[here] = product(z_low.at[here], left, lower).astype(BF16)
    second[...] = product(weights, left, lower)
    cells_x, cells_y = inner.shape[:2]
    start = 0
    for volume in (first, second):
        where = pl.ds(start, volume.shape[1])
        start += volume.shape[1]
        place = lax.broadcasted_iota(jnp.int32, (cells_y, volume.shape[1]), 0)
        for x in range(cells_x):
            row = lambda k: volume[pl.ds(k * cells_y, cells_y)]
            here = row(x)
            around_it = jnp.where(place == 0, 0.0, pltpu.roll(here, 1, 0)) + jnp.where(
                place == cells_y - 1, 0.0, pltpu.roll(here, cells_y - 1, 0)
            )
            if x:
                around_it = around_it + row(x - 1)
            if x + 1 < cells_x:
                around_it = around_it + row(x + 1)
            scale = wavenum[pl.ds(x * cells_y, cells_y)][:, :1]
            inner[x, :, where] = around_it - 4.0 * here + scale * here
    for copy in copies:
        copy.wait()


def plain(z_top, z_low, weights, left, lower, wavenum, volume, before, cells_y):
    trace, width = lower.shape
    cells = volume.shape[0]
    total = before.shape[1]
    given = 7
    return pl.pallas_call(
        plain_kernel,
        out_shape=(
            jax.ShapeDtypeStruct(before.shape, before.dtype),
            jax.ShapeDtypeStruct((cells // cells_y, cells_y, total), F32),
            jax.ShapeDtypeStruct((trace, width), BF16),
        ),
        in_specs=[VMEM] * given + [HBM],
        out_specs=(HBM, VMEM, VMEM),
        scratch_shapes=[
            pltpu.VMEM((trace, width), BF16),
            pltpu.VMEM((cells, width), F32),
            pltpu.SemaphoreType.DMA((2,)),
        ],
        input_output_aliases={given: 0},
        cost_estimate=cost(8 * trace * trace * width, 8 * trace * trace + 8 * trace * width),
        compiler_params=PACKED,
        name="plain",
    )(z_top, z_low, weights, left, lower, wavenum, volume, before)


def beside(axis, pair, cross):
    place = lax.axis_index(axis)
    even = lax.rem(place, 2) == 0
    pair, cross = pair[...].astype(F32), cross[...].astype(F32)
    before = jnp.where(place == 0, 0.0, jnp.where(even, cross, pair))
    after = jnp.where(is_last(axis), 0.0, jnp.where(even, pair, cross))
    return before, after


def finish_kernel(inner, upper, x_pair, x_cross, y_pair, y_cross, _, upper_hbm, residual_hbm, out, sem):
    cells_x, cells_y, total = inner.shape
    groups = sem.shape[0] - 1
    deep = cells_x // groups
    before_x, after_x = beside("gx", x_pair, x_cross)
    before_y, after_y = beside("gy", y_pair, y_cross)
    place = lax.broadcasted_iota(jnp.int32, (cells_y, total), 0)
    width = upper.shape[1]
    base = upper_hbm.shape[1] - width
    copies = [pltpu.make_async_copy(upper, upper_hbm.at[:, pl.ds(base, width)], sem.at[groups])]
    copies[0].start()
    for group in range(groups):
        for x in range(group * deep, (group + 1) * deep):
            value = inner[x]
            value = value + jnp.where(
                place == 0, before_y[x : x + 1], jnp.where(place == cells_y - 1, after_y[x : x + 1], 0.0)
            )
            if x == 0:
                value = value + before_x
            if x == cells_x - 1:
                value = value + after_x
            out[x] = value
        here = pl.ds(group * deep, deep)
        copies.append(pltpu.make_async_copy(out.at[here], residual_hbm.at[here], sem.at[group]))
        copies[-1].start()
    for copy in copies:
        copy.wait()


def finish(inner, upper, halos, before):
    groups = 1
    given = 2 + len(halos)
    return pl.pallas_call(
        finish_kernel,
        out_shape=(jax.ShapeDtypeStruct(before.shape, before.dtype), jax.ShapeDtypeStruct(inner.shape, F32)),
        in_specs=[VMEM] * given + [HBM],
        out_specs=(HBM, HBM),
        scratch_shapes=[pltpu.VMEM(inner.shape, F32), pltpu.SemaphoreType.DMA((groups + 1,))],
        input_output_aliases={given: 0},
        cost_estimate=cost(4 * inner.size, 8 * inner.size),
        compiler_params=PARAMS,
        name="finish",
    )(inner, upper, *halos, before)


def per_device(impedance, rebuild_map, left_trace, lower_trace, cell_kind, kind_wavenum):
    z = pltpu.with_memory_space_constraint(impedance[0, 0], pltpu.HBM)
    weights = rebuild_map[0, 0]
    left_all = pltpu.with_memory_space_constraint(left_trace[0, 0], pltpu.HBM)
    lower_all = pltpu.with_memory_space_constraint(lower_trace[0, 0], pltpu.HBM)
    sources = left_all.shape[1]
    width = sources // CHUNKS
    _, cells_y = cell_kind.shape
    left_in, lower_in = [None] * CHUNKS, [None] * CHUNKS
    for step in range(STEPS - 1):
        for c in range(CHUNKS):
            if step == 0 and c == 0:
                right, z_top, left, lower = first_right(z, left_all, lower_all, 0, width)
            elif step == 0:
                right, left, lower = part_loading("gx", z_top, left_all, lower_all, c * width, width)
            else:
                left, lower = left_in[c], lower_in[c]
                right = part("gx", z_top, left, lower)
            final = step == STEPS - 2 and c == CHUNKS - 1
            left_in[c] = onward(right, "gx") if final else around(right, "gx")
            if step == 0 and c == 0:
                upper, z_low = first_upper(z, left, lower)
            else:
                upper = part("gy", z_low, left, lower)
            lower_in[c] = around(upper, "gy")

    wavenum = wavenum_of(kind_wavenum, cell_kind)
    volume, edges, edge_weights = volume_of(weights, left_in[0], lower_in[0], cells_y)
    outs = last(z_top, z_low, left_in[0], lower_in[0], sources)
    volume, wavenum, left, lower, *outs = lax.optimization_barrier(
        (volume, wavenum, left_in[1], lower_in[1], *outs)
    )
    x_pair, x_cross, y_pair, y_cross = edges_of(edge_weights, left, lower, edges, cells_y)
    x_pair = swapped(x_pair, "gx", 0)
    x_cross = swapped(x_cross, "gx", 1)
    y_cross = swapped(y_cross, "gy", 1)
    y_pair = swapped(y_pair, "gy", 0)
    halos = (x_pair, x_cross, y_pair, y_cross)
    right_out, inner, upper = plain(z_top, z_low, weights, left, lower, wavenum, volume, outs[0], cells_y)
    upper_out, residual = finish(inner, upper, halos, outs[1])
    return (right_out[None, None], upper_out[None, None], residual)


def solution(mesh):
    return jax.shard_map(
        per_device,
        mesh=mesh,
        in_specs=(
            P("gx", "gy", None, None),
            P("gx", "gy", None, None),
            P("gx", "gy", None, None),
            P("gx", "gy", None, None),
            P("gx", "gy"),
            P(),
        ),
        out_specs=(P("gx", "gy", None, None), P("gx", "gy", None, None), P("gx", "gy", None)),
        check_vma=False,
    )
```
